128 devices in a mesh: tm: 8 (over x, z_hi), rows: 16 (over z_lo, y, core).
Axes of the slice: x: 4, y: 4, z: 4 (z_hi: 2, z_lo: 2; z = z_hi * 2 + z_lo), core: 2. Of those that a mesh axis runs over, the one named last changes fastest.
Arguments:
- heights: bfloat16 [256, 1024, 1024], P('tm', 'rows'), may hold values from -6 to 6
Outputs:
- spectrum: float32 [64, 1024, 1024], P(None, ('tm', 'rows'))
The draws below stay inside these ranges and needn't reach their ends.
All inputs are finite; a program needn't handle non-finite values.
Results may differ from the reference program's by a relative error of at most 0.0035.
Values may be sent and summed in bfloat16 or wider, within the bound.
A program may use at most 128 MiB of HBM per device.

```python
import math
import jax
import jax.numpy as jnp
from jax import lax

GRID = 1024
WIN = 64
FRAMES = 256


def level_of(stream_key, shape, cuts, smallest, largest):
    def one(axis_at, blocks):
        draws = jax.random.uniform(jax.random.fold_in(jax.random.fold_in(stream_key, 6), axis_at), (blocks,), jnp.float32, smallest / len(cuts), largest / len(cuts))
        return jnp.repeat(jnp.exp(draws), shape[axis_at] // blocks).reshape((-1,) + (1,) * (len(shape) - axis_at - 1))

    level = one(*cuts[0])
    for cut in cuts[1:]:
        level = level * one(*cut)
    return level


def centred(key, shape, width, reach, pieces=(), kind=jnp.bfloat16):
    factor_of = level_of(key, shape, pieces, -0.22, 0.18) if pieces else 1.0
    drawn = jax.random.normal(key, shape, jnp.float32) * width * factor_of
    return jnp.minimum(jnp.maximum(drawn, -reach), reach).astype(kind)


def setup_inputs(seed: int = 0) -> dict:
    streams_of = jax.random.split(jax.random.key(seed), 2)
    return {
        "heights": centred(streams_of[0], (FRAMES, GRID, GRID), 1.0, 6.0, ((0, 8), (1, 16))),
    }


def spatial_table(length):
    column = jnp.arange(2 * length, dtype=jnp.int32)
    column_part = column % 2
    wavenumber = column // 2
    position = jnp.arange(length, dtype=jnp.int32)
    angles = (position[:, None] * wavenumber[None, :] % length).astype(jnp.float32) * (2.0 * math.pi / length)
    values = jnp.where(column_part[None, :] == 0, jnp.cos(angles), -jnp.sin(angles))
    return (values / math.sqrt(length)).astype(jnp.bfloat16)

def make_column_table(length):
    position = jnp.arange(length, dtype=jnp.int32)
    angles = (position[:, None] * position[None, :] % length).astype(jnp.float32) * (2.0 * math.pi / length)
    values = jnp.concatenate([jnp.cos(angles), jnp.sin(angles)], 1)
    return (values / math.sqrt(length)).astype(jnp.bfloat16)

def time_table(window_len):
    time_step = jnp.arange(window_len, dtype=jnp.int32)
    hann_taper = 0.5 - 0.5 * jnp.cos(time_step.astype(jnp.float32) * (2.0 * math.pi / window_len))
    angles = (time_step[:, None] * time_step[None, :] % window_len).astype(jnp.float32) * (2.0 * math.pi / window_len)
    tables = jnp.stack([jnp.cos(angles) * hann_taper[None, :], jnp.sin(angles) * hann_taper[None, :]], 0)
    return (tables.astype(jnp.bfloat16), jnp.sum(hann_taper * hann_taper))

def window_power(window, time_taper):
    number = window.shape[2]
    length = window.shape[3]
    block_size = math.gcd(number, 64)

    def one_block(block_index, accumulated):
        slab_piece = lax.dynamic_slice_in_dim(window, block_index * block_size, block_size, 2)
        product = jnp.einsum('swt,tpqx->swpqx', time_taper.astype(jnp.float32), slab_piece.astype(jnp.float32))
        real_part = product[0, :, 0] + product[1, :, 1]
        imag_part = product[0, :, 1] - product[1, :, 0]
        return lax.dynamic_update_slice_in_dim(accumulated, real_part * real_part + imag_part * imag_part, block_index * block_size, 1)
    start = jnp.zeros((time_taper.shape[1], number, length), jnp.float32)
    return lax.fori_loop(0, number // block_size, one_block, start)

def reference(heights):
    number = heights.shape[0]
    length = heights.shape[1]
    row_table = spatial_table(length).astype(jnp.float32)
    col_table = make_column_table(length).astype(jnp.float32)
    time_taper, energy = time_table(WIN)
    hop_size = WIN // 2

    def frame_modes(single_frame):
        mixed_rows = jnp.dot(single_frame.astype(jnp.float32), row_table, preferred_element_type=jnp.float32).astype(jnp.bfloat16)
        product = jnp.dot(mixed_rows.T.astype(jnp.float32), col_table, preferred_element_type=jnp.float32)
        product = product.reshape(length, 2, 2, length)
        real_part = product[:, 0, 0] + product[:, 1, 1]
        imag_part = product[:, 1, 0] - product[:, 0, 1]
        return jnp.stack([real_part, imag_part], 0).astype(jnp.bfloat16)

    def block_modes(block_index):
        frame_block = lax.dynamic_slice_in_dim(heights, block_index * hop_size, hop_size, 0)
        return lax.map(frame_modes, frame_block)
    first_block = block_modes(jnp.int32(0))

    def advance(state_pair, block_index):
        previous, summed = state_pair
        current = block_modes(block_index)
        summed = summed + window_power(jnp.concatenate([previous, current], 0), time_taper)
        return ((current, summed), None)
    start = jnp.zeros((WIN, length, length), jnp.float32)
    (last_block, summed), unused = lax.scan(advance, (first_block, start), jnp.arange(1, number // hop_size, dtype=jnp.int32))
    return summed / ((number // hop_size - 1) * energy)
```

```python
import functools
import math

import jax
import jax.numpy as jnp
import ml_dtypes
import numpy as np
from jax import lax
from jax.experimental import pallas as pl
from jax.experimental.pallas import tpu as pltpu
from jax.sharding import PartitionSpec as P

MESH = pl.DeviceIdType.MESH
GRID = 1024
HALF = 512
WIN = 64
TM = 8
ROWS = 16
DEVICES = TM * ROWS
FRAMES_DEV = 32
X_DEV = 64
BF16 = jnp.bfloat16
F32 = jnp.float32


def trig(index):
    angles = (index % GRID).astype(np.float32) * np.float32(2.0 * math.pi / GRID)
    scale = np.float32(math.sqrt(GRID))
    return np.cos(angles) / scale, np.sin(angles) / scale


def row_table():
    row = np.arange(HALF)
    pair, part, parity, low = row // 8, row // 4 % 2, row // 2 % 2, row % 2
    device = 2 * pair + parity
    y = np.arange(HALF)
    tables = []
    for phase in range(2):
        slot = 2 * phase + low
        q = np.where(device < 64, 8 * device + slot, 8 * (127 - device) + 4 + slot)
        cosine, sine = trig(q[:, None] * y[None, :])
        values = np.where(part[:, None] == 0, cosine, -sine)
        shared = (device == 0) & (slot == 0) & (part == 1)
        nyquist, _ = trig(HALF * y)
        tables.append(np.where(shared[:, None], nyquist[None, :], values))
    return np.stack(tables).astype(ml_dtypes.bfloat16)


def column_table():
    x = np.arange(HALF)
    cosine, sine = trig(x[:, None] * x[None, :])
    sine[:, 0] = trig(x * HALF)[0]
    return np.concatenate([cosine, sine], 1).astype(ml_dtypes.bfloat16)


def tapers():
    t = np.arange(WIN)
    hann = np.float32(0.5) - np.float32(0.5) * np.cos(
        t.astype(np.float32) * np.float32(2.0 * math.pi / WIN)
    )
    angles = (t[:, None] * t[None, :] % WIN).astype(np.float32) * np.float32(2.0 * math.pi / WIN)
    energy = float(np.sum(hann * hann, dtype=np.float32))

    def rounded(values):
        return (values * hann[None, :]).astype(ml_dtypes.bfloat16).astype(np.float32)

    return rounded(np.cos(angles)), rounded(np.sin(angles)), energy


def time_matrices():
    cosine, sine, _ = tapers()
    k = np.arange(256)
    block, second, inner = k // 128, k // 64 % 2, k // 16 % 4
    high, part, low, slot = k // 8 % 2, k // 4 % 2, k // 2 % 2, k % 2
    t = 32 * block + 8 * (2 * high + low) + 2 * inner + second
    real = np.where(part == 0, cosine[:, t], sine[:, t])
    imag = np.where(part == 0, -sine[:, t], cosine[:, t])
    rows = [np.where(slot == s, m, 0.0) for s in range(2) for m in (real, imag)]
    back = (-np.arange(WIN)) % WIN
    first = rows[:2] + [rows[0][back], rows[1][back]]
    return (
        np.concatenate(rows).astype(ml_dtypes.bfloat16),
        np.concatenate(first).astype(ml_dtypes.bfloat16),
    )


def peer_of(step, tm, rows):
    x, z = tm // 2, (tm % 2) * 2 + rows // 8
    y, core = rows // 2 % 4, rows % 2
    shift = step * 91 % DEVICES
    x = (x + shift // 32) % 4
    y = (y + shift // 8 % 4) % 4
    z = (z + shift // 2 % 4) % 4
    core = (core + shift % 2) % 2
    return x * 2 + z // 2, (z % 2 * 4 + y) * 2 + core


def spectrum_kernel(
    h_ref, ty_ref, tx_ref, time_ref, time0_ref, own_ref, got_ref,
    tab, txa, txb, rowsum, send, recv, lhs, rc, rs, modes, msg,
    send_sem, recv_sem, local_sem, msg_send_sem, msg_recv_sem,
):
    tm, rows = lax.axis_index("tm"), lax.axis_index("rows")
    me = tm * ROWS + rows
    core = rows % 2

    def device(target):
        return {"tm": target // ROWS, "rows": target % ROWS}

    barrier = pltpu.get_barrier_semaphore()

    @pl.loop(1, DEVICES)
    def _(step):
        pl.semaphore_signal(
            barrier, inc=1, device_id=device((me + step) % DEVICES), device_id_type=MESH
        )

    row_sign = jnp.where(lax.broadcasted_iota(jnp.int32, (HALF, 1), 0) % 2 == 0, 1.0, -1.0)
    for phase in range(2):
        tab[phase, :, :HALF] = ty_ref[phase]
        tab[phase, :, HALF:] = (ty_ref[phase].astype(F32) * row_sign).astype(BF16)
    lane_sign = jnp.where(lax.broadcasted_iota(jnp.int32, (1, GRID), 1) % 2 == 0, 1.0, -1.0)
    txa[:HALF] = tx_ref[...]
    txa[HALF:] = (tx_ref[...].astype(F32) * lane_sign).astype(BF16)

    @pl.loop(0, 8)
    def _(block):
        base = pl.multiple_of(block * 128, 128)
        txb[pl.ds(base, 64)] = txa[pl.ds(base + 64, 64)]
        txb[pl.ds(base + 64, 64)] = txa[pl.ds(base, 64)]

    def row_phase(phase):
        for inner in range(2):
            lanes = slice(inner * 256, inner * 256 + 256)

            @pl.loop(0, 4)
            def _(quarter):
                base = quarter * 8 + inner * 4
                block = jnp.concatenate(
                    [
                        h_ref[base + core],
                        h_ref[base + 1 - core],
                        h_ref[base + 2 + core],
                        h_ref[base + 3 - core],
                    ],
                    0,
                )
                rowsum[quarter] = lax.dot_general(
                    tab[phase], block, (((1,), (1,)), ((), ())), preferred_element_type=F32
                )

            @pl.loop(0, 8)
            def _(part):
                at = pl.ds(pl.multiple_of(part * 64, 64), 64)
                pieces = [rowsum[f, at].reshape(8, 8, 256) for f in range(4)]
                early = lax.broadcasted_iota(jnp.int32, (8, 8, 256), 1) // 2 % 2 == 0
                evens, odds = [], []
                for a, b in ((pieces[0], pieces[1]), (pieces[2], pieces[3])):
                    evens.append(jnp.where(early, a, pltpu.roll(b, 2, 1)))
                    odds.append(jnp.where(early, pltpu.roll(a, 6, 1), b))
                pairs = pl.ds(part * 8, 8)
                send[phase, pairs, 0, :, lanes] = jnp.concatenate(evens, 1).astype(BF16)
                send[phase, pairs, 1, :, lanes] = jnp.concatenate(odds, 1).astype(BF16)

    def start_sends(phase):
        @pl.loop(1, DEVICES)
        def _(step):
            to_tm, to_rows = peer_of(step, tm, rows)
            target = to_tm * ROWS + to_rows
            pltpu.make_async_remote_copy(
                src_ref=send.at[phase, target // 2, target % 2],
                dst_ref=recv.at[phase, me],
                send_sem=send_sem.at[phase],
                recv_sem=recv_sem.at[phase],
                device_id={"tm": to_tm, "rows": to_rows},
                device_id_type=MESH,
            ).start()

        pltpu.make_async_copy(
            send.at[phase, me // 2, me % 2], recv.at[phase, me], local_sem.at[phase]
        ).start()

    def wait_all(phase, sem):
        blocks = recv.at[phase, pl.ds(0, DEVICES - 1)]
        pltpu.make_async_copy(blocks, blocks, sem.at[phase]).wait()

    def column_phase(phase):
        @pl.loop(0, TM)
        def _(block):
            low = lax.broadcasted_iota(jnp.int32, (16, 512), 1) % 128 < 64
            for pair in range(8):
                even = recv[phase, block * ROWS + 2 * pair]
                odd = recv[phase, block * ROWS + 2 * pair + 1]
                first = jnp.where(low, even, odd)
                second = jnp.where(low, odd, even)
                for inner in range(4):
                    at = pl.ds(pl.multiple_of(block * 64 + inner * 16, 16), 16)
                    lanes = slice(inner * 128, inner * 128 + 128)
                    columns = slice(pair * 128, pair * 128 + 128)
                    lhs[0, at, columns] = first[:, lanes]
                    lhs[1, at, columns] = second[:, lanes]

        for second in range(2):
            table = txb if second else txa
            for part in range(2):
                columns = slice(part * 256, part * 256 + 256)
                above = slice(HALF + part * 256, HALF + part * 256 + 256)
                rc[...] = jnp.dot(lhs[second], table[:, columns], preferred_element_type=F32)
                rs[...] = jnp.dot(lhs[second], table[:, above], preferred_element_type=F32)

                @pl.loop(0, TM)
                def _(block):
                    at = pl.ds(pl.multiple_of(block * 64, 64), 64)
                    cosine = rc[at].reshape(8, 8, 256)
                    sine = rs[at].reshape(8, 8, 256)
                    top = lax.broadcasted_iota(jnp.int32, (8, 8, 256), 1) < 4
                    swapped = pltpu.roll(sine, 4, 1)
                    swapped = jnp.where(top, swapped, -swapped)
                    plus, minus = cosine + swapped, cosine - swapped
                    if part == 0:
                        edge = lax.broadcasted_iota(jnp.int32, (8, 8, 256), 2) == 0
                        plus = jnp.where(edge, cosine, plus)
                        minus = jnp.where(edge, sine, minus)
                    modes[block, second, :, columns] = plus.reshape(64, 256).astype(BF16)
                    modes[block, second, :, above] = minus.reshape(64, 256).astype(BF16)

    def time_phase(phase):
        @pl.loop(0, 4)
        def _(part):
            columns = pl.ds(pl.multiple_of(part * 256, 256), 256)
            total = None
            for window in range(TM - 1):
                u = jnp.dot(
                    time_ref[...],
                    modes[pl.ds(window, 2), :, :, columns].reshape(256, 256),
                    preferred_element_type=F32,
                )
                u = u * u
                power = jnp.concatenate([u[:64] + u[64:128], u[128:192] + u[192:]], 0)
                total = power if total is None else total + power
            for low in range(2):
                piece = total[low * 64 : low * 64 + 64]
                own_ref[2 * phase + low, :, columns] = piece
                msg[2 * phase + low, :, columns] = piece.astype(BF16)

        if phase == 0:
            @pl.when(me == 0)
            def _():
                @pl.loop(0, 2)
                def _(part):
                    columns = pl.ds(pl.multiple_of(part * 256, 256), 256)
                    above = pl.ds(pl.multiple_of(HALF + part * 256, 256), 256)
                    lane = lax.broadcasted_iota(jnp.int32, (128, 256), 1) + part * 256
                    sums = [None] * 4
                    for window in range(TM - 1):
                        a, b = (
                            jnp.dot(
                                time0_ref[...],
                                modes[pl.ds(window, 2), :, :, at].reshape(256, 256),
                                preferred_element_type=F32,
                            )
                            for at in (columns, above)
                        )
                        back_a = jnp.where(lane == 0, a[128:], b[128:])
                        back_b = jnp.where(lane == 0, b[128:], a[128:])
                        terms = []
                        for here, back in ((a[:128], back_a), (b[:128], back_b)):
                            r, i, rb, ib = here[:64], here[64:], back[:64], back[64:]
                            terms.append((r + rb) * (r + rb) + (i - ib) * (i - ib))
                            terms.append((r - rb) * (r - rb) + (i + ib) * (i + ib))
                        sums = [t if s is None else s + t for s, t in zip(sums, terms)]
                    own_ref[0, :, columns] = sums[0] * 0.25
                    own_ref[0, :, above] = sums[2] * 0.25
                    msg[0, :, columns] = (sums[1] * 0.25).astype(BF16)
                    msg[0, :, above] = (sums[3] * 0.25).astype(BF16)

    mirror = DEVICES - 1 - me
    first_to = jnp.where(me == 0, 64, jnp.where(me < 64, DEVICES - me, mirror))

    def message(slot):
        return pltpu.make_async_remote_copy(
            src_ref=msg.at[slot],
            dst_ref=got_ref.at[slot],
            send_sem=msg_send_sem.at[slot],
            recv_sem=msg_recv_sem.at[slot],
            device_id=device(first_to if slot == 0 else mirror),
            device_id_type=MESH,
        )

    row_phase(0)
    pl.semaphore_wait(barrier, DEVICES - 1)
    start_sends(0)
    row_phase(1)
    start_sends(1)
    for phase in range(2):
        pltpu.make_async_copy(
            send.at[phase, me // 2, me % 2], recv.at[phase, me], local_sem.at[phase]
        ).wait()
        wait_all(phase, recv_sem)
        column_phase(phase)
        time_phase(phase)
        for low in range(2):
            message(2 * phase + low).start()
    for phase in range(2):
        wait_all(phase, send_sem)
    for slot in range(4):
        message(slot).wait()


def final_kernel(scale, own_ref, got_ref, out_ref, stack, left, flip):
    me = lax.axis_index("tm") * ROWS + lax.axis_index("rows")
    upper = me >= 64
    i = lax.broadcasted_iota(jnp.int32, (HALF, HALF), 0)
    j = lax.broadcasted_iota(jnp.int32, (HALF, HALF), 1)
    flip[...] = jnp.where(i == (HALF - j) % HALF, 1.0, 0.0).astype(BF16)
    to = lax.broadcasted_iota(jnp.int32, (HALF, 256), 0)
    come = lax.broadcasted_iota(jnp.int32, (HALF, 256), 1)
    w, row = to // 8, to % 8
    w_from = jnp.where(upper, (WIN - w) % WIN, w)
    slot_own = jnp.where(upper, jnp.where((row >= 1) & (row <= 4), 4 - row, -1), jnp.where(row < 4, row, -1))
    slot_got = jnp.where(
        upper, jnp.where(row == 0, 0, jnp.where(row >= 5, 8 - row, -1)), jnp.where(row >= 4, row - 4, -1)
    )
    own_map = jnp.where((come // WIN == slot_own) & (come % WIN == w_from), 1.0, 0.0).astype(BF16)
    left[:, :256] = own_map
    left[:, 256:512] = own_map
    left[:, 512:] = jnp.where((come // WIN == slot_got) & (come % WIN == w_from), 1.0, 0.0).astype(BF16)
    swap = (lax.broadcasted_iota(jnp.int32, (256, HALF), 1) >= 1) & upper

    def place(at, a, b):
        stack[at, :HALF] = jnp.where(swap, b, a).astype(BF16)
        other = jnp.where(swap, a, b).astype(BF16)
        stack[at, HALF:] = jnp.dot(other, flip[...], preferred_element_type=F32).astype(BF16)

    a, b = own_ref[:, :HALF], own_ref[:, HALF:]
    a_top, b_top = a.astype(BF16).astype(F32), b.astype(BF16).astype(F32)
    place(slice(0, 256), a_top, b_top)
    place(slice(256, 512), a - a_top, b - b_top)
    place(slice(512, 768), got_ref[:, :HALF].astype(F32), got_ref[:, HALF:].astype(F32))

    for part in range(4):
        columns = slice(part * 256, part * 256 + 256)
        result = jnp.dot(left[...], stack[:, columns], preferred_element_type=F32) * scale
        out_ref[:, :, columns] = result.reshape(WIN, 8, 256)


def body(heights):
    vmem = pl.BlockSpec(memory_space=pltpu.VMEM)
    time_matrix, time_first = time_matrices()
    energy = tapers()[2]
    dma = pltpu.SemaphoreType.DMA
    own, got = pl.pallas_call(
        spectrum_kernel,
        out_shape=(
            jax.ShapeDtypeStruct((4, WIN, GRID), F32),
            jax.ShapeDtypeStruct((4, WIN, GRID), BF16),
        ),
        in_specs=[vmem] * 5,
        out_specs=(vmem, vmem),
        scratch_shapes=[
            pltpu.VMEM((2, HALF, GRID), BF16),
            pltpu.VMEM((GRID, GRID), BF16),
            pltpu.VMEM((GRID, GRID), BF16),
            pltpu.VMEM((4, HALF, 256), F32),
            pltpu.VMEM((2, DEVICES // 2, 2, 16, 512), BF16),
            pltpu.VMEM((2, DEVICES, 16, 512), BF16),
            pltpu.VMEM((2, HALF, GRID), BF16),
            pltpu.VMEM((HALF, 256), F32),
            pltpu.VMEM((HALF, 256), F32),
            pltpu.VMEM((TM, 2, 64, GRID), BF16),
            pltpu.VMEM((4, WIN, GRID), BF16),
            dma((2,)),
            dma((2,)),
            dma((2,)),
            dma((4,)),
            dma((4,)),
        ],
        compiler_params=pltpu.CompilerParams(
            collective_id=0, has_side_effects=True, vmem_limit_bytes=60 << 20
        ),
    )(
        heights,
        jnp.asarray(row_table()),
        jnp.asarray(column_table()),
        jnp.asarray(time_matrix),
        jnp.asarray(time_first),
    )
    return pl.pallas_call(
        functools.partial(final_kernel, 1.0 / ((TM - 1) * energy)),
        out_shape=jax.ShapeDtypeStruct((WIN, 8, GRID), F32),
        in_specs=[vmem, vmem],
        out_specs=vmem,
        scratch_shapes=[
            pltpu.VMEM((768, GRID), BF16),
            pltpu.VMEM((HALF, 768), BF16),
            pltpu.VMEM((HALF, HALF), BF16),
        ],
        compiler_params=pltpu.CompilerParams(vmem_limit_bytes=40 << 20),
    )(own.reshape(256, GRID), got.reshape(256, GRID))


def solution(mesh):
    return jax.shard_map(
        body,
        mesh=mesh,
        in_specs=(P("tm", "rows", None),),
        out_specs=P(None, ("tm", "rows"), None),
        check_vma=False,
    )
```

```python
import functools
import math

import jax
import jax.numpy as jnp
import ml_dtypes
import numpy as np
from jax import lax
from jax.experimental import pallas as pl
from jax.experimental.pallas import tpu as pltpu
from jax.sharding import PartitionSpec as P

MESH = pl.DeviceIdType.MESH
GRID = 1024
HALF = 512
WIN = 64
TM = 8
ROWS = 16
DEVICES = TM * ROWS
FRAMES_DEV = 32
X_DEV = 64
VMEM_ALL = 67_000_000
BF16 = jnp.bfloat16
F32 = jnp.float32


def trig(index):
    angles = (index % GRID).astype(np.float32) * np.float32(2.0 * math.pi / GRID)
    scale = np.float32(math.sqrt(GRID))
    return np.cos(angles) / scale, np.sin(angles) / scale


def row_table():
    row = np.arange(HALF)
    pair, part, parity, low = row // 8, row // 4 % 2, row // 2 % 2, row % 2
    device = 2 * pair + parity
    y = np.arange(HALF)
    tables = []
    for phase in range(2):
        slot = 2 * phase + low
        q = np.where(device < 64, 8 * device + slot, 8 * (127 - device) + 4 + slot)
        cosine, sine = trig(q[:, None] * y[None, :])
        values = np.where(part[:, None] == 0, cosine, -sine)
        shared = (device == 0) & (slot == 0) & (part == 1)
        nyquist, _ = trig(HALF * y)
        tables.append(np.where(shared[:, None], nyquist[None, :], values))
    return np.stack(tables).astype(ml_dtypes.bfloat16)


def column_table():
    x = np.arange(HALF)
    cosine, sine = trig(x[:, None] * x[None, :])
    sine[:, 0] = trig(x * HALF)[0]
    return np.concatenate([cosine, sine], 1).astype(ml_dtypes.bfloat16)


def tapers():
    t = np.arange(WIN)
    hann = np.float32(0.5) - np.float32(0.5) * np.cos(
        t.astype(np.float32) * np.float32(2.0 * math.pi / WIN)
    )
    angles = (t[:, None] * t[None, :] % WIN).astype(np.float32) * np.float32(2.0 * math.pi / WIN)
    energy = float(np.sum(hann * hann, dtype=np.float32))

    def rounded(values):
        return (values * hann[None, :]).astype(ml_dtypes.bfloat16).astype(np.float32)

    return rounded(np.cos(angles)), rounded(np.sin(angles)), energy


def time_matrices():
    cosine, sine, _ = tapers()
    k = np.arange(256)
    block, second, inner = k // 128, k // 64 % 2, k // 16 % 4
    high, part, low, slot = k // 8 % 2, k // 4 % 2, k // 2 % 2, k % 2
    t = 32 * block + 8 * (2 * high + low) + 2 * inner + second
    real = np.where(part == 0, cosine[:, t], sine[:, t])
    imag = np.where(part == 0, -sine[:, t], cosine[:, t])
    rows = [np.where(slot == s, m, 0.0) for s in range(2) for m in (real, imag)]
    back = (-np.arange(WIN)) % WIN
    first = rows[:2] + [rows[0][back], rows[1][back]]
    return (
        np.concatenate(rows).astype(ml_dtypes.bfloat16),
        np.concatenate(first).astype(ml_dtypes.bfloat16),
    )


def peer_of(step, tm, rows):
    x, z = tm // 2, (tm % 2) * 2 + rows // 8
    y, core = rows // 2 % 4, rows % 2
    shift = step * 91 % DEVICES
    x = (x + shift // 32) % 4
    y = (y + shift // 8 % 4) % 4
    z = (z + shift // 2 % 4) % 4
    core = (core + shift % 2) % 2
    return x * 2 + z // 2, (z % 2 * 4 + y) * 2 + core


def far(step):
    a, b = step // ROWS, step % ROWS
    return min(a // 2, 4 - a // 2) + a % 2 * 2 + b // 8 + min(b // 2 % 4, 4 - b // 2 % 4)


def spectrum_kernel(
    h_hbm, ty_hbm, tx_hbm, time_ref, time0_ref, own_hbm, got_ref,
    h_ref, ty_ref, tx_ref, own_ref, tab, txa, txb, rowsum, send, recv, lhs, rc, rs, modes, msg,
    send_sem, recv_sem, local_sem, msg_send_sem, msg_recv_sem, load_sem, own_sem,
):
    tm, rows = lax.axis_index("tm"), lax.axis_index("rows")
    me = tm * ROWS + rows
    core = rows % 2

    def device(target):
        return {"tm": target // ROWS, "rows": target % ROWS}

    loads = [
        pltpu.make_async_copy(source, target, load_sem.at[i])
        for i, (source, target) in enumerate(
            ((ty_hbm, ty_ref), (h_hbm, h_ref), (tx_hbm, tx_ref))
        )
    ]
    for load in loads:
        load.start()

    barrier = pltpu.get_barrier_semaphore()
    tm_of = [(tm + a) % TM for a in range(TM)]
    rows_of = [(rows + b) % ROWS for b in range(ROWS)]
    for step in sorted(range(1, DEVICES), key=far, reverse=True):
        pl.semaphore_signal(
            barrier,
            inc=1,
            device_id={"tm": tm_of[step // ROWS], "rows": rows_of[step % ROWS]},
            device_id_type=MESH,
        )

    loads[0].wait()
    row_sign = jnp.where(lax.broadcasted_iota(jnp.int32, (HALF, 1), 0) % 2 == 0, 1.0, -1.0)
    for phase in range(2):
        tab[phase, :, :HALF] = ty_ref[phase]
        tab[phase, :, HALF:] = (ty_ref[phase].astype(F32) * row_sign).astype(BF16)
    def column_tables():
        lane_sign = jnp.where(lax.broadcasted_iota(jnp.int32, (1, GRID), 1) % 2 == 0, 1.0, -1.0)
        txa[:HALF] = tx_ref[...]
        txa[HALF:] = (tx_ref[...].astype(F32) * lane_sign).astype(BF16)

        @pl.loop(0, 8)
        def _(block):
            base = pl.multiple_of(block * 128, 128)
            txb[pl.ds(base, 64)] = txa[pl.ds(base + 64, 64)]
            txb[pl.ds(base + 64, 64)] = txa[pl.ds(base, 64)]

    def row_phase(phase):
        for inner in range(2):
            lanes = slice(inner * 256, inner * 256 + 256)

            @pl.loop(0, 4)
            def _(quarter):
                base = quarter * 8 + inner * 4
                block = jnp.concatenate(
                    [
                        h_ref[base + core],
                        h_ref[base + 1 - core],
                        h_ref[base + 2 + core],
                        h_ref[base + 3 - core],
                    ],
                    0,
                )
                rowsum[quarter] = lax.dot_general(
                    tab[phase], block, (((1,), (1,)), ((), ())), preferred_element_type=F32
                )

            @pl.loop(0, 8)
            def _(part):
                at = pl.ds(pl.multiple_of(part * 64, 64), 64)
                pieces = [rowsum[f, at].reshape(8, 8, 256) for f in range(4)]
                early = lax.broadcasted_iota(jnp.int32, (8, 8, 256), 1) // 2 % 2 == 0
                evens, odds = [], []
                for a, b in ((pieces[0], pieces[1]), (pieces[2], pieces[3])):
                    evens.append(jnp.where(early, a, pltpu.roll(b, 2, 1)))
                    odds.append(jnp.where(early, pltpu.roll(a, 6, 1), b))
                pairs = pl.ds(part * 8, 8)
                send[phase, pairs, 0, :, lanes] = jnp.concatenate(evens, 1).astype(BF16)
                send[phase, pairs, 1, :, lanes] = jnp.concatenate(odds, 1).astype(BF16)

    def start_sends(phase):
        @pl.loop(1, DEVICES)
        def _(step):
            to_tm, to_rows = peer_of(step, tm, rows)
            target = to_tm * ROWS + to_rows
            pltpu.make_async_remote_copy(
                src_ref=send.at[phase, target // 2, target % 2],
                dst_ref=recv.at[phase, me],
                send_sem=send_sem.at[phase],
                recv_sem=recv_sem.at[phase],
                device_id={"tm": to_tm, "rows": to_rows},
                device_id_type=MESH,
            ).start()

        pltpu.make_async_copy(
            send.at[phase, me // 2, me % 2], recv.at[phase, me], local_sem.at[phase]
        ).start()

    def wait_all(phase, sem):
        blocks = recv.at[phase, pl.ds(0, DEVICES - 1)]
        pltpu.make_async_copy(blocks, blocks, sem.at[phase]).wait()

    def column_phase(phase):
        @pl.loop(0, TM)
        def _(block):
            low = lax.broadcasted_iota(jnp.int32, (16, 512), 1) % 128 < 64
            for pair in range(8):
                even = recv[phase, block * ROWS + 2 * pair]
                odd = recv[phase, block * ROWS + 2 * pair + 1]
                first = jnp.where(low, even, odd)
                second = jnp.where(low, odd, even)
                for inner in range(4):
                    at = pl.ds(pl.multiple_of(block * 64 + inner * 16, 16), 16)
                    lanes = slice(inner * 128, inner * 128 + 128)
                    columns = slice(pair * 128, pair * 128 + 128)
                    lhs[0, at, columns] = first[:, lanes]
                    lhs[1, at, columns] = second[:, lanes]

        for second in range(2):
            table = txb if second else txa
            for part in range(2):
                columns = slice(part * 256, part * 256 + 256)
                above = slice(HALF + part * 256, HALF + part * 256 + 256)
                rc[...] = jnp.dot(lhs[second], table[:, columns], preferred_element_type=F32)
                rs[...] = jnp.dot(lhs[second], table[:, above], preferred_element_type=F32)

                @pl.loop(0, TM)
                def _(block):
                    at = pl.ds(pl.multiple_of(block * 64, 64), 64)
                    cosine = rc[at].reshape(8, 8, 256)
                    sine = rs[at].reshape(8, 8, 256)
                    top = lax.broadcasted_iota(jnp.int32, (8, 8, 256), 1) < 4
                    swapped = pltpu.roll(sine, 4, 1)
                    swapped = jnp.where(top, swapped, -swapped)
                    plus, minus = cosine + swapped, cosine - swapped
                    if part == 0:
                        edge = lax.broadcasted_iota(jnp.int32, (8, 8, 256), 2) == 0
                        plus = jnp.where(edge, cosine, plus)
                        minus = jnp.where(edge, sine, minus)
                    modes[block, second, :, columns] = plus.reshape(64, 256).astype(BF16)
                    modes[block, second, :, above] = minus.reshape(64, 256).astype(BF16)

    def time_phase(phase):
        @pl.loop(0, 4)
        def _(part):
            columns = pl.ds(pl.multiple_of(part * 256, 256), 256)
            total = None
            for window in range(TM - 1):
                u = jnp.dot(
                    time_ref[...],
                    modes[pl.ds(window, 2), :, :, columns].reshape(256, 256),
                    preferred_element_type=F32,
                )
                u = u * u
                power = jnp.concatenate([u[:64] + u[64:128], u[128:192] + u[192:]], 0)
                total = power if total is None else total + power
            for low in range(2):
                piece = total[low * 64 : low * 64 + 64]
                own_ref[2 * phase + low, :, columns] = piece
                msg[2 * phase + low, :, columns] = piece.astype(BF16)

        if phase == 0:
            @pl.when(me == 0)
            def _():
                @pl.loop(0, 2)
                def _(part):
                    columns = pl.ds(pl.multiple_of(part * 256, 256), 256)
                    above = pl.ds(pl.multiple_of(HALF + part * 256, 256), 256)
                    lane = lax.broadcasted_iota(jnp.int32, (128, 256), 1) + part * 256
                    sums = [None] * 4
                    for window in range(TM - 1):
                        a, b = (
                            jnp.dot(
                                time0_ref[...],
                                modes[pl.ds(window, 2), :, :, at].reshape(256, 256),
                                preferred_element_type=F32,
                            )
                            for at in (columns, above)
                        )
                        back_a = jnp.where(lane == 0, a[128:], b[128:])
                        back_b = jnp.where(lane == 0, b[128:], a[128:])
                        terms = []
                        for here, back in ((a[:128], back_a), (b[:128], back_b)):
                            r, i, rb, ib = here[:64], here[64:], back[:64], back[64:]
                            terms.append((r + rb) * (r + rb) + (i - ib) * (i - ib))
                            terms.append((r - rb) * (r - rb) + (i + ib) * (i + ib))
                        sums = [t if s is None else s + t for s, t in zip(sums, terms)]
                    own_ref[0, :, columns] = sums[0] * 0.25
                    own_ref[0, :, above] = sums[2] * 0.25
                    msg[0, :, columns] = (sums[1] * 0.25).astype(BF16)
                    msg[0, :, above] = (sums[3] * 0.25).astype(BF16)

    mirror = DEVICES - 1 - me
    first_to = jnp.where(me == 0, 64, jnp.where(me < 64, DEVICES - me, mirror))

    def own_copy(phase):
        slots = pl.ds(2 * phase, 2)
        return pltpu.make_async_copy(own_ref.at[slots], own_hbm.at[slots], own_sem.at[phase])

    def message(slot):
        return pltpu.make_async_remote_copy(
            src_ref=msg.at[slot],
            dst_ref=got_ref.at[slot],
            send_sem=msg_send_sem.at[slot],
            recv_sem=msg_recv_sem.at[slot],
            device_id=device(first_to if slot == 0 else mirror),
            device_id_type=MESH,
        )

    loads[1].wait()
    row_phase(0)
    pl.semaphore_wait(barrier, DEVICES - 1)
    start_sends(0)
    row_phase(1)
    start_sends(1)
    loads[2].wait()
    column_tables()
    for phase in range(2):
        pltpu.make_async_copy(
            send.at[phase, me // 2, me % 2], recv.at[phase, me], local_sem.at[phase]
        ).wait()
        wait_all(phase, recv_sem)
        column_phase(phase)
        time_phase(phase)
        for low in range(2):
            message(2 * phase + low).start()
        own_copy(phase).start()
    for phase in range(2):
        wait_all(phase, send_sem)
    for phase in range(2):
        own_copy(phase).wait()
    for slot in range(4):
        message(slot).wait()


def final_kernel(
    scale, own_hbm, got_hbm, out_hbm, own_ref, got_ref, stack, left, flip, result, in_sem, out_sem
):
    loads = [
        pltpu.make_async_copy(own_hbm, own_ref, in_sem.at[0]),
        pltpu.make_async_copy(got_hbm, got_ref, in_sem.at[1]),
    ]
    for load in loads:
        load.start()
    me = lax.axis_index("tm") * ROWS + lax.axis_index("rows")
    upper = me >= 64
    i = lax.broadcasted_iota(jnp.int32, (HALF, HALF), 0)
    j = lax.broadcasted_iota(jnp.int32, (HALF, HALF), 1)
    flip[...] = jnp.where(i == (HALF - j) % HALF, 1.0, 0.0).astype(BF16)
    to = lax.broadcasted_iota(jnp.int32, (HALF, 256), 0)
    come = lax.broadcasted_iota(jnp.int32, (HALF, 256), 1)
    w, row = to // 8, to % 8
    w_from = jnp.where(upper, (WIN - w) % WIN, w)
    slot_own = jnp.where(
        upper, jnp.where((row >= 1) & (row <= 4), 4 - row, -1), jnp.where(row < 4, row, -1)
    )
    slot_got = jnp.where(
        upper,
        jnp.where(row == 0, 0, jnp.where(row >= 5, 8 - row, -1)),
        jnp.where(row >= 4, row - 4, -1),
    )
    own_map = jnp.where(come == slot_own * WIN + w_from, 1.0, 0.0).astype(BF16)
    left[:, :256] = own_map
    left[:, 256:512] = own_map
    left[:, 512:] = jnp.where(come == slot_got * WIN + w_from, 1.0, 0.0).astype(BF16)
    swap = (lax.broadcasted_iota(jnp.int32, (256, HALF), 1) >= 1) & upper

    def place(at, a, b):
        stack[at, :HALF] = jnp.where(swap, b, a).astype(BF16)
        other = jnp.where(swap, a, b).astype(BF16)
        stack[at, HALF:] = jnp.dot(other, flip[...], preferred_element_type=F32).astype(BF16)

    loads[0].wait()
    a, b = own_ref[:, :HALF], own_ref[:, HALF:]
    a_top, b_top = a.astype(BF16).astype(F32), b.astype(BF16).astype(F32)
    place(slice(0, 256), a_top, b_top)
    place(slice(256, 512), a - a_top, b - b_top)
    loads[1].wait()
    place(slice(512, 768), got_ref[:, :HALF].astype(F32), got_ref[:, HALF:].astype(F32))

    stores = []
    for part in range(4):
        columns = slice(part * 256, part * 256 + 256)
        product = jnp.dot(left[...], stack[:, columns], preferred_element_type=F32) * scale
        result[part] = product.reshape(WIN, 8, 256)
        store = pltpu.make_async_copy(
            result.at[part], out_hbm.at[:, :, pl.ds(part * 256, 256)], out_sem.at[part]
        )
        store.start()
        stores.append(store)
    for store in stores:
        store.wait()


def body(heights):
    vmem = pl.BlockSpec(memory_space=pltpu.VMEM)
    hbm = pl.BlockSpec(memory_space=pl.ANY)
    time_matrix, time_first = time_matrices()
    energy = tapers()[2]
    dma = pltpu.SemaphoreType.DMA
    own, got = pl.pallas_call(
        spectrum_kernel,
        out_shape=(
            jax.ShapeDtypeStruct((4, WIN, GRID), F32),
            jax.ShapeDtypeStruct((4, WIN, GRID), BF16),
        ),
        in_specs=[hbm] * 3 + [vmem] * 2,
        out_specs=(hbm, hbm),
        scratch_shapes=[
            pltpu.VMEM((FRAMES_DEV, X_DEV, GRID), BF16),
            pltpu.VMEM((2, HALF, HALF), BF16),
            pltpu.VMEM((HALF, GRID), BF16),
            pltpu.VMEM((4, WIN, GRID), F32),
            pltpu.VMEM((2, HALF, GRID), BF16),
            pltpu.VMEM((GRID, GRID), BF16),
            pltpu.VMEM((GRID, GRID), BF16),
            pltpu.VMEM((4, HALF, 256), F32),
            pltpu.VMEM((2, DEVICES // 2, 2, 16, 512), BF16),
            pltpu.VMEM((2, DEVICES, 16, 512), BF16),
            pltpu.VMEM((2, HALF, GRID), BF16),
            pltpu.VMEM((HALF, 256), F32),
            pltpu.VMEM((HALF, 256), F32),
            pltpu.VMEM((TM, 2, 64, GRID), BF16),
            pltpu.VMEM((4, WIN, GRID), BF16),
            dma((2,)),
            dma((2,)),
            dma((2,)),
            dma((4,)),
            dma((4,)),
            dma((3,)),
            dma((2,)),
        ],
        compiler_params=pltpu.CompilerParams(
            collective_id=0, has_side_effects=True, vmem_limit_bytes=VMEM_ALL
        ),
    )(
        heights,
        jnp.asarray(row_table()),
        jnp.asarray(column_table()),
        jnp.asarray(time_matrix),
        jnp.asarray(time_first),
    )
    return pl.pallas_call(
        functools.partial(final_kernel, 1.0 / ((TM - 1) * energy)),
        out_shape=jax.ShapeDtypeStruct((WIN, 8, GRID), F32),
        in_specs=[hbm, hbm],
        out_specs=hbm,
        scratch_shapes=[
            pltpu.VMEM((256, GRID), F32),
            pltpu.VMEM((256, GRID), BF16),
            pltpu.VMEM((768, GRID), BF16),
            pltpu.VMEM((HALF, 768), BF16),
            pltpu.VMEM((HALF, HALF), BF16),
            pltpu.VMEM((4, WIN, 8, 256), F32),
            dma((2,)),
            dma((4,)),
        ],
        compiler_params=pltpu.CompilerParams(vmem_limit_bytes=VMEM_ALL),
    )(own.reshape(256, GRID), got.reshape(256, GRID))


def solution(mesh):
    return jax.shard_map(
        body,
        mesh=mesh,
        in_specs=(P("tm", "rows", None),),
        out_specs=P(None, ("tm", "rows"), None),
        check_vma=False,
    )
```

```python
import functools
import math

import jax
import jax.numpy as jnp
import ml_dtypes
import numpy as np
from jax import lax
from jax.experimental import pallas as pl
from jax.experimental.pallas import tpu as pltpu
from jax.sharding import PartitionSpec as P

MESH = pl.DeviceIdType.MESH
GRID = 1024
HALF = 512
WIN = 64
TM = 8
ROWS = 16
DEVICES = TM * ROWS
FRAMES_DEV = 32
X_DEV = 64
SLOTS = 4
QUARTER = 256
VMEM_ALL = 67_000_000
BF16 = jnp.bfloat16
F32 = jnp.float32


def trig(index):
    angles = (index % GRID).astype(np.float32) * np.float32(2.0 * math.pi / GRID)
    scale = np.float32(math.sqrt(GRID))
    return np.cos(angles) / scale, np.sin(angles) / scale


def row_table():
    row = np.arange(QUARTER)
    quad, part, low = row // 8, row // 4 % 2, row % 4
    device = 4 * quad + low
    y = np.arange(HALF)
    tables = []
    for slot in range(SLOTS):
        q = np.where(device < 64, 8 * device + slot, 8 * (127 - device) + 4 + slot)
        cosine, sine = trig(q[:, None] * y[None, :])
        values = np.where(part[:, None] == 0, cosine, -sine)
        shared = (device == 0) & (slot == 0) & (part == 1)
        nyquist, _ = trig(HALF * y)
        tables.append(np.where(shared[:, None], nyquist[None, :], values))
    return np.stack(tables).astype(ml_dtypes.bfloat16)


def column_table():
    x = np.arange(HALF)
    cosine, sine = trig(x[:, None] * x[None, :])
    sine[:, 0] = trig(x * HALF)[0]
    return np.concatenate([cosine, sine], 1).astype(ml_dtypes.bfloat16)


def tapers():
    t = np.arange(WIN)
    hann = np.float32(0.5) - np.float32(0.5) * np.cos(
        t.astype(np.float32) * np.float32(2.0 * math.pi / WIN)
    )
    angles = (t[:, None] * t[None, :] % WIN).astype(np.float32) * np.float32(2.0 * math.pi / WIN)
    energy = float(np.sum(hann * hann, dtype=np.float32))

    def rounded(values):
        return (values * hann[None, :]).astype(ml_dtypes.bfloat16).astype(np.float32)

    return rounded(np.cos(angles)), rounded(np.sin(angles)), energy


def time_matrices():
    cosine, sine, _ = tapers()
    k = np.arange(128)
    block, second, inner = k // 64, k // 32 % 2, k // 16 % 2
    high, part, low = k // 8 % 2, k // 4 % 2, k % 4
    t = 32 * block + 16 * high + 4 * low + 2 * inner + second
    real = np.where(part == 0, cosine[:, t], sine[:, t])
    imag = np.where(part == 0, -sine[:, t], cosine[:, t])
    back = (-np.arange(WIN)) % WIN
    return np.concatenate([real, imag, real[back], imag[back]]).astype(ml_dtypes.bfloat16)


def far(step):
    a, b = step // ROWS, step % ROWS
    return min(a // 2, 4 - a // 2) + a % 2 * 2 + b // 8 + min(b // 2 % 4, 4 - b // 2 % 4)


def spectrum_kernel(
    h_hbm, ty_hbm, tx_hbm, time_ref, own_hbm, got_hbm,
    h_ref, ty_ref, tx_ref, own_ref, tab, txa, txb, rowsum, send, recv, lhs, rc, rs, modes, msg,
    send_sem, recv_sem, local_sem, msg_send_sem, msg_recv_sem, load_sem, own_sem,
):
    tm, rows = lax.axis_index("tm"), lax.axis_index("rows")
    me = tm * ROWS + rows
    x, y, z, core = tm // 2, rows // 2 % 4, tm % 2 * 2 + rows // 8, rows % 2

    loads = [
        pltpu.make_async_copy(source, target, load_sem.at[i])
        for i, (source, target) in enumerate(
            ((ty_hbm, ty_ref), (h_hbm, h_ref), (tx_hbm, tx_ref))
        )
    ]
    for load in loads:
        load.start()

    barrier = pltpu.get_barrier_semaphore()
    tm_of = [(tm + a) % TM for a in range(TM)]
    rows_of = [(rows + b) % ROWS for b in range(ROWS)]
    for step in sorted(range(1, DEVICES), key=far, reverse=True):
        pl.semaphore_signal(
            barrier,
            inc=1,
            device_id={"tm": tm_of[step // ROWS], "rows": rows_of[step % ROWS]},
            device_id_type=MESH,
        )

    def row_tables(slot):
        tab[slot, :, :HALF] = ty_ref[slot]
        tab[slot, :, HALF:] = -ty_ref[slot] if slot % 2 else ty_ref[slot]

    def column_tables():
        lane_sign = jnp.where(lax.broadcasted_iota(jnp.int32, (1, GRID), 1) % 2 == 0, 1.0, -1.0)
        txa[:HALF] = tx_ref[...]
        txa[HALF:] = (tx_ref[...].astype(F32) * lane_sign).astype(BF16)

        @pl.loop(0, 8)
        def _(block):
            base = pl.multiple_of(block * 128, 128)
            txb[pl.ds(base, 64)] = txa[pl.ds(base + 64, 64)]
            txb[pl.ds(base + 64, 64)] = txa[pl.ds(base, 64)]

    def row_phase(slot):
        @pl.loop(0, 8)
        def _(eighth):
            base = eighth * 4
            block = jnp.concatenate(
                [
                    h_ref[base + core],
                    h_ref[base + 1 - core],
                    h_ref[base + 2 + core],
                    h_ref[base + 3 - core],
                ],
                0,
            )
            rowsum[eighth] = lax.dot_general(
                tab[slot], block, (((1,), (1,)), ((), ())), preferred_element_type=F32
            )

        @pl.loop(0, 8)
        def _(part):
            at = pl.ds(pl.multiple_of(part * 32, 32), 32)
            row = lax.broadcasted_iota(jnp.int32, (4, 8, 256), 1)
            pair, single = row // 2 % 2 == 0, row % 2 == 0
            halves = []
            for high in range(2):
                r = [rowsum[4 * high + f, at].reshape(4, 8, 256) for f in range(4)]
                a = [None] * 4
                for f in range(2):
                    a[f] = jnp.where(pair, r[f], pltpu.roll(r[f + 2], 2, 1))
                    a[f + 2] = jnp.where(pair, pltpu.roll(r[f], 6, 1), r[f + 2])
                halves.append(
                    [
                        jnp.where(single, a[0], pltpu.roll(a[1], 1, 1)),
                        jnp.where(single, pltpu.roll(a[0], 7, 1), a[1]),
                        jnp.where(single, a[2], pltpu.roll(a[3], 1, 1)),
                        jnp.where(single, pltpu.roll(a[2], 7, 1), a[3]),
                    ]
                )
            for low in range(4):
                send[slot, pl.ds(part * 4, 4), low] = jnp.concatenate(
                    [halves[0][low], halves[1][low]], 1
                ).astype(BF16)

    def start_sends(slot):
        y_of = [(y + d) % 4 * 2 for d in range(4)]
        z_of = [(z + d) % 4 for d in range(4)]
        z_tm, z_rows = [v // 2 for v in z_of], [v % 2 * 8 for v in z_of]
        core_of = [core, 1 - core]

        @pl.loop(0, 4)
        def _(turn):
            x_of = [(x + 3 * turn + d) % 4 * 2 for d in range(4)]

            def start(step):
                shift = step * 91 % DEVICES
                to_tm = x_of[shift // 32] + z_tm[shift // 2 % 4]
                to_rows = z_rows[shift // 2 % 4] + y_of[shift // 8 % 4] + core_of[shift % 2]
                target = to_tm * ROWS + to_rows
                pltpu.make_async_remote_copy(
                    src_ref=send.at[slot, target // 4, target % 4],
                    dst_ref=recv.at[slot, me],
                    send_sem=send_sem.at[slot],
                    recv_sem=recv_sem.at[slot],
                    device_id={"tm": to_tm, "rows": to_rows},
                    device_id_type=MESH,
                ).start()

            @pl.when(turn > 0)
            def _():
                start(0)

            for step in range(1, 32):
                start(step)

        local_copy(slot).start()

    def local_copy(slot):
        return pltpu.make_async_copy(
            send.at[slot, me // 4, me % 4], recv.at[slot, me], local_sem.at[slot]
        )

    def wait_all(slot, sem):
        blocks = recv.at[slot, pl.ds(0, DEVICES - 1)]
        pltpu.make_async_copy(blocks, blocks, sem.at[slot]).wait()

    def gather_phase(slot):
        @pl.loop(0, TM)
        def _(block):
            low = lax.broadcasted_iota(jnp.int32, (16, 256), 1) % 128 < 64
            for pair in range(8):
                even = recv[slot, block * ROWS + 2 * pair]
                odd = recv[slot, block * ROWS + 2 * pair + 1]
                first = jnp.where(low, even, odd)
                second = jnp.where(low, odd, even)
                for inner in range(2):
                    at = pl.ds(pl.multiple_of(block * 32 + inner * 16, 16), 16)
                    lanes = slice(inner * 128, inner * 128 + 128)
                    columns = slice(pair * 128, pair * 128 + 128)
                    lhs[0, at, columns] = first[:, lanes]
                    lhs[1, at, columns] = second[:, lanes]

    def column_phase(part):
        columns = slice(part * 256, part * 256 + 256)
        above = slice(HALF + part * 256, HALF + part * 256 + 256)
        for second in range(2):
            table = txb if second else txa
            rc[...] = jnp.dot(lhs[second], table[:, columns], preferred_element_type=F32)
            rs[...] = jnp.dot(lhs[second], table[:, above], preferred_element_type=F32)

            @pl.loop(0, TM)
            def _(block):
                at = pl.ds(pl.multiple_of(block * 32, 32), 32)
                cosine = rc[at].reshape(4, 8, 256)
                sine = rs[at].reshape(4, 8, 256)
                top = lax.broadcasted_iota(jnp.int32, (4, 8, 256), 1) < 4
                swapped = pltpu.roll(sine, 4, 1)
                swapped = jnp.where(top, swapped, -swapped)
                plus, minus = cosine + swapped, cosine - swapped
                if part == 0:
                    edge = lax.broadcasted_iota(jnp.int32, (4, 8, 256), 2) == 0
                    plus = jnp.where(edge, cosine, plus)
                    minus = jnp.where(edge, sine, minus)
                modes[block, second, :, columns] = plus.reshape(32, 256).astype(BF16)
                modes[block, second, :, above] = minus.reshape(32, 256).astype(BF16)

    def window_at(window, columns):
        return modes[pl.ds(window, 2), :, :, columns].reshape(128, 256)

    def time_phase(slot, part):
        for half in range(2):
            columns = slice(half * HALF + part * 256, half * HALF + part * 256 + 256)
            total = None
            for window in range(TM - 1):
                u = jnp.dot(
                    time_ref[:128], window_at(window, columns), preferred_element_type=F32
                )
                u = u * u
                power = u[:64] + u[64:]
                total = power if total is None else total + power
            own_ref[slot, :, columns] = total
            msg[slot, part, :, half * 256 : half * 256 + 256] = total.astype(BF16)

        @pl.when((me == 0) & (slot == 0))
        def _():
            columns = slice(part * 256, part * 256 + 256)
            above = slice(HALF + part * 256, HALF + part * 256 + 256)
            lane = lax.broadcasted_iota(jnp.int32, (128, 256), 1) + part * 256
            sums = [None] * 4
            for window in range(TM - 1):
                a, b = (
                    jnp.dot(time_ref[...], window_at(window, at), preferred_element_type=F32)
                    for at in (columns, above)
                )
                back_a = jnp.where(lane == 0, a[128:], b[128:])
                back_b = jnp.where(lane == 0, b[128:], a[128:])
                terms = []
                for here, back in ((a[:128], back_a), (b[:128], back_b)):
                    r, i, rb, ib = here[:64], here[64:], back[:64], back[64:]
                    terms.append((r + rb) * (r + rb) + (i - ib) * (i - ib))
                    terms.append((r - rb) * (r - rb) + (i + ib) * (i + ib))
                sums = [t if s is None else s + t for s, t in zip(sums, terms)]
            own_ref[0, :, columns] = sums[0] * 0.25
            own_ref[0, :, above] = sums[2] * 0.25
            msg[0, part, :, :256] = (sums[1] * 0.25).astype(BF16)
            msg[0, part, :, 256:] = (sums[3] * 0.25).astype(BF16)

    def own_copy(slot):
        return pltpu.make_async_copy(own_ref.at[slot], own_hbm.at[slot], own_sem.at[slot])

    mirror = DEVICES - 1 - me
    first_to = jnp.where(me == 0, 64, jnp.where(me < 64, DEVICES - me, mirror))

    def message(slot, part):
        target = jnp.where(slot == 0, first_to, mirror)
        return pltpu.make_async_remote_copy(
            src_ref=msg.at[slot, part],
            dst_ref=got_hbm.at[slot, part],
            send_sem=msg_send_sem.at[slot, part],
            recv_sem=msg_recv_sem.at[slot, part],
            device_id={"tm": target // ROWS, "rows": target % ROWS},
            device_id_type=MESH,
        )

    loads[0].wait()
    row_tables(0)
    loads[1].wait()
    row_phase(0)
    pl.semaphore_wait(barrier, DEVICES - 1)
    for slot in range(1, SLOTS):
        row_tables(slot)

    @pl.loop(0, SLOTS)
    def _(slot):
        start_sends(slot)

        @pl.when(slot < SLOTS - 1)
        def _():
            row_phase(slot + 1)

    loads[2].wait()
    column_tables()

    @pl.loop(0, SLOTS)
    def _(slot):
        local_copy(slot).wait()
        wait_all(slot, recv_sem)
        gather_phase(slot)
        for part in range(2):
            column_phase(part)
            time_phase(slot, part)
            message(slot, part).start()
        own_copy(slot).start()

    @pl.loop(0, SLOTS)
    def _(slot):
        wait_all(slot, send_sem)
        own_copy(slot).wait()
        for part in range(2):
            message(slot, part).wait()


def final_kernel(
    scale, own_hbm, got_hbm, out_hbm, own_ref, got_ref, stack, left, flip, result, in_sem, out_sem
):
    loads = [
        pltpu.make_async_copy(own_hbm, own_ref, in_sem.at[0]),
        pltpu.make_async_copy(got_hbm, got_ref, in_sem.at[1]),
    ]
    for load in loads:
        load.start()
    me = lax.axis_index("tm") * ROWS + lax.axis_index("rows")
    upper = me >= 64
    i = lax.broadcasted_iota(jnp.int32, (HALF, HALF), 0)
    j = lax.broadcasted_iota(jnp.int32, (HALF, HALF), 1)
    flip[...] = jnp.where(i == (HALF - j) % HALF, 1.0, 0.0).astype(BF16)
    to = lax.broadcasted_iota(jnp.int32, (HALF, 256), 0)
    come = lax.broadcasted_iota(jnp.int32, (HALF, 256), 1)
    w, row = to // 8, to % 8
    w_from = jnp.where(upper, (WIN - w) % WIN, w)
    slot_own = jnp.where(
        upper, jnp.where((row >= 1) & (row <= 4), 4 - row, -1), jnp.where(row < 4, row, -1)
    )
    slot_got = jnp.where(
        upper,
        jnp.where(row == 0, 0, jnp.where(row >= 5, 8 - row, -1)),
        jnp.where(row >= 4, row - 4, -1),
    )
    own_map = jnp.where(come == slot_own * WIN + w_from, 1.0, 0.0).astype(BF16)
    left[:, :256] = own_map
    left[:, 256:512] = own_map
    left[:, 512:] = jnp.where(come == slot_got * WIN + w_from, 1.0, 0.0).astype(BF16)
    swap = (lax.broadcasted_iota(jnp.int32, (256, HALF), 1) >= 1) & upper

    def place(at, a, b):
        stack[at, :HALF] = jnp.where(swap, b, a).astype(BF16)
        other = jnp.where(swap, a, b).astype(BF16)
        stack[at, HALF:] = jnp.dot(other, flip[...], preferred_element_type=F32).astype(BF16)

    loads[0].wait()
    a, b = own_ref[:, :HALF], own_ref[:, HALF:]
    a_top, b_top = a.astype(BF16).astype(F32), b.astype(BF16).astype(F32)
    place(slice(0, 256), a_top, b_top)
    place(slice(256, 512), a - a_top, b - b_top)
    loads[1].wait()
    halves = [
        jnp.concatenate(
            [got_ref[:, part, :, at].reshape(256, 256).astype(F32) for part in range(2)], 1
        )
        for at in (slice(0, 256), slice(256, 512))
    ]
    place(slice(512, 768), *halves)

    stores = []
    for part in range(4):
        columns = slice(part * 256, part * 256 + 256)
        product = jnp.dot(left[...], stack[:, columns], preferred_element_type=F32) * scale
        result[part] = product.reshape(WIN, 8, 256)
        store = pltpu.make_async_copy(
            result.at[part], out_hbm.at[:, :, pl.ds(part * 256, 256)], out_sem.at[part]
        )
        store.start()
        stores.append(store)
    for store in stores:
        store.wait()


def body(heights):
    vmem = pl.BlockSpec(memory_space=pltpu.VMEM)
    hbm = pl.BlockSpec(memory_space=pl.ANY)
    energy = tapers()[2]
    dma = pltpu.SemaphoreType.DMA
    own, got = pl.pallas_call(
        spectrum_kernel,
        out_shape=(
            jax.ShapeDtypeStruct((SLOTS, WIN, GRID), F32),
            jax.ShapeDtypeStruct((SLOTS, 2, WIN, HALF), BF16),
        ),
        in_specs=[hbm] * 3 + [vmem],
        out_specs=(hbm, hbm),
        scratch_shapes=[
            pltpu.VMEM((FRAMES_DEV, X_DEV, GRID), BF16),
            pltpu.VMEM((SLOTS, QUARTER, HALF), BF16),
            pltpu.VMEM((HALF, GRID), BF16),
            pltpu.VMEM((SLOTS, WIN, GRID), F32),
            pltpu.VMEM((SLOTS, QUARTER, GRID), BF16),
            pltpu.VMEM((GRID, GRID), BF16),
            pltpu.VMEM((GRID, GRID), BF16),
            pltpu.VMEM((8, QUARTER, 256), F32),
            pltpu.VMEM((SLOTS, DEVICES // 4, 4, 16, 256), BF16),
            pltpu.VMEM((SLOTS, DEVICES, 16, 256), BF16),
            pltpu.VMEM((2, QUARTER, GRID), BF16),
            pltpu.VMEM((QUARTER, 256), F32),
            pltpu.VMEM((QUARTER, 256), F32),
            pltpu.VMEM((TM, 2, 32, GRID), BF16),
            pltpu.VMEM((SLOTS, 2, WIN, HALF), BF16),
            dma((SLOTS,)),
            dma((SLOTS,)),
            dma((SLOTS,)),
            dma((SLOTS, 2)),
            dma((SLOTS, 2)),
            dma((3,)),
            dma((SLOTS,)),
        ],
        compiler_params=pltpu.CompilerParams(
            collective_id=0, has_side_effects=True, vmem_limit_bytes=VMEM_ALL
        ),
    )(
        heights,
        jnp.asarray(row_table()),
        jnp.asarray(column_table()),
        jnp.asarray(time_matrices()),
    )
    return pl.pallas_call(
        functools.partial(final_kernel, 1.0 / ((TM - 1) * energy)),
        out_shape=jax.ShapeDtypeStruct((WIN, 8, GRID), F32),
        in_specs=[hbm, hbm],
        out_specs=hbm,
        scratch_shapes=[
            pltpu.VMEM((256, GRID), F32),
            pltpu.VMEM((SLOTS, 2, WIN, HALF), BF16),
            pltpu.VMEM((768, GRID), BF16),
            pltpu.VMEM((HALF, 768), BF16),
            pltpu.VMEM((HALF, HALF), BF16),
            pltpu.VMEM((4, WIN, 8, 256), F32),
            dma((2,)),
            dma((4,)),
        ],
        compiler_params=pltpu.CompilerParams(vmem_limit_bytes=VMEM_ALL),
    )(own.reshape(256, GRID), got)


def solution(mesh):
    return jax.shard_map(
        body,
        mesh=mesh,
        in_specs=(P("tm", "rows", None),),
        out_specs=P(None, ("tm", "rows"), None),
        check_vma=False,
    )
```

```python
import functools
import math

import jax
import jax.numpy as jnp
import ml_dtypes
import numpy as np
from jax import lax
from jax.experimental import pallas as pl
from jax.experimental.pallas import tpu as pltpu
from jax.sharding import PartitionSpec as P

MESH = pl.DeviceIdType.MESH
GRID = 1024
HALF = 512
WIN = 64
TM = 8
ROWS = 16
DEVICES = TM * ROWS
FRAMES_DEV = 32
X_DEV = 64
SLOTS = 4
QUARTER = 256
VMEM_ALL = 67_000_000
BF16 = jnp.bfloat16
F32 = jnp.float32


def trig(index):
    angles = (index % GRID).astype(np.float32) * np.float32(2.0 * math.pi / GRID)
    scale = np.float32(math.sqrt(GRID))
    return np.cos(angles) / scale, np.sin(angles) / scale


def row_table():
    row = np.arange(QUARTER)
    quad, part, low = row // 8, row // 4 % 2, row % 4
    device = 4 * quad + low
    y = np.arange(HALF)
    tables = []
    for slot in range(SLOTS):
        q = np.where(device < 64, 8 * device + slot, 8 * (127 - device) + 4 + slot)
        cosine, sine = trig(q[:, None] * y[None, :])
        values = np.where(part[:, None] == 0, cosine, -sine)
        shared = (device == 0) & (slot == 0) & (part == 1)
        nyquist, _ = trig(HALF * y)
        tables.append(np.where(shared[:, None], nyquist[None, :], values))
    return np.stack(tables).astype(ml_dtypes.bfloat16)


def column_table():
    x = np.arange(HALF)
    cosine, sine = trig(x[:, None] * x[None, :])
    sine[:, 0] = trig(x * HALF)[0]
    return np.concatenate([cosine, sine], 1).astype(ml_dtypes.bfloat16)


def tapers():
    t = np.arange(WIN)
    hann = np.float32(0.5) - np.float32(0.5) * np.cos(
        t.astype(np.float32) * np.float32(2.0 * math.pi / WIN)
    )
    angles = (t[:, None] * t[None, :] % WIN).astype(np.float32) * np.float32(2.0 * math.pi / WIN)
    energy = float(np.sum(hann * hann, dtype=np.float32))

    def rounded(values):
        return (values * hann[None, :]).astype(ml_dtypes.bfloat16).astype(np.float32)

    return rounded(np.cos(angles)), rounded(np.sin(angles)), energy


def time_matrices():
    cosine, sine, _ = tapers()
    k = np.arange(128)
    block, second, inner = k // 64, k // 32 % 2, k // 16 % 2
    high, part, low = k // 8 % 2, k // 4 % 2, k % 4
    t = 32 * block + 16 * high + 4 * low + 2 * inner + second
    real = np.where(part == 0, cosine[:, t], sine[:, t])
    imag = np.where(part == 0, -sine[:, t], cosine[:, t])
    back = (-np.arange(WIN)) % WIN
    return np.concatenate([real, imag, real[back], imag[back]]).astype(ml_dtypes.bfloat16)


def far(step):
    a, b = step // ROWS, step % ROWS
    return min(a // 2, 4 - a // 2) + a % 2 * 2 + b // 8 + min(b // 2 % 4, 4 - b // 2 % 4)


def make_flip(flip):
    i = lax.broadcasted_iota(jnp.int32, (HALF, HALF), 0)
    j = lax.broadcasted_iota(jnp.int32, (HALF, HALF), 1)
    flip[...] = jnp.where(i == (HALF - j) % HALF, 1.0, 0.0).astype(BF16)


def spectrum_kernel(
    h_hbm, ty_hbm, tx_hbm, time_ref, own_hbm, got_hbm,
    h_ref, ty_ref, tx_ref, own_ref, tab, txa, txb, rowsum, send, recv, lhs, rc, rs, modes, msg, stack, flip,
    send_sem, recv_sem, local_sem, msg_send_sem, msg_recv_sem, load_sem, height_sem, own_sem,
):
    tm, rows = lax.axis_index("tm"), lax.axis_index("rows")
    me = tm * ROWS + rows
    x, y, z, core = tm // 2, rows // 2 % 4, tm % 2 * 2 + rows // 8, rows % 2

    def height_load(eighth):
        frames = pl.ds(eighth * 4, 4)
        return pltpu.make_async_copy(h_hbm.at[frames], h_ref.at[frames], height_sem.at[eighth])

    later = pl.ds(1, SLOTS - 1)
    loads = [
        pltpu.make_async_copy(ty_hbm.at[0], ty_ref.at[0], load_sem.at[0]),
        pltpu.make_async_copy(ty_hbm.at[later], ty_ref.at[later], load_sem.at[1]),
        pltpu.make_async_copy(tx_hbm, tx_ref, load_sem.at[2]),
    ]
    loads[0].start()
    for eighth in range(8):
        height_load(eighth).start()
    loads[1].start()
    loads[2].start()

    barrier = pltpu.get_barrier_semaphore()
    tm_of = [(tm + a) % TM for a in range(TM)]
    rows_of = [(rows + b) % ROWS for b in range(ROWS)]
    for step in sorted(range(1, DEVICES), key=far, reverse=True):
        pl.semaphore_signal(
            barrier,
            inc=1,
            device_id={"tm": tm_of[step // ROWS], "rows": rows_of[step % ROWS]},
            device_id_type=MESH,
        )

    def row_tables(slot):
        tab[slot, :, :HALF] = ty_ref[slot]
        tab[slot, :, HALF:] = -ty_ref[slot] if slot % 2 else ty_ref[slot]

    def column_tables():
        lane_sign = jnp.where(lax.broadcasted_iota(jnp.int32, (1, GRID), 1) % 2 == 0, 1.0, -1.0)
        txa[:HALF] = tx_ref[...]
        txa[HALF:] = (tx_ref[...].astype(F32) * lane_sign).astype(BF16)

        @pl.loop(0, 8)
        def _(block):
            base = pl.multiple_of(block * 128, 128)
            txb[pl.ds(base, 64)] = txa[pl.ds(base + 64, 64)]
            txb[pl.ds(base + 64, 64)] = txa[pl.ds(base, 64)]

    def row_phase(slot):
        first = isinstance(slot, int)

        @pl.loop(0, 8)
        def _(eighth):
            if first:
                height_load(eighth).wait()
            base = eighth * 4
            block = jnp.concatenate(
                [
                    h_ref[base + core],
                    h_ref[base + 1 - core],
                    h_ref[base + 2 + core],
                    h_ref[base + 3 - core],
                ],
                0,
            )
            rowsum[eighth] = lax.dot_general(
                tab[slot], block, (((1,), (1,)), ((), ())), preferred_element_type=F32
            )

        @pl.loop(0, 8)
        def _(part):
            at = pl.ds(pl.multiple_of(part * 32, 32), 32)
            row = lax.broadcasted_iota(jnp.int32, (4, 8, 256), 1)
            pair, single = row // 2 % 2 == 0, row % 2 == 0
            halves = []
            for high in range(2):
                r = [rowsum[4 * high + f, at].reshape(4, 8, 256) for f in range(4)]
                a = [None] * 4
                for f in range(2):
                    a[f] = jnp.where(pair, r[f], pltpu.roll(r[f + 2], 2, 1))
                    a[f + 2] = jnp.where(pair, pltpu.roll(r[f], 6, 1), r[f + 2])
                halves.append(
                    [
                        jnp.where(single, a[0], pltpu.roll(a[1], 1, 1)),
                        jnp.where(single, pltpu.roll(a[0], 7, 1), a[1]),
                        jnp.where(single, a[2], pltpu.roll(a[3], 1, 1)),
                        jnp.where(single, pltpu.roll(a[2], 7, 1), a[3]),
                    ]
                )
            for low in range(4):
                send[slot, pl.ds(part * 4, 4), low] = jnp.concatenate(
                    [halves[0][low], halves[1][low]], 1
                ).astype(BF16)

    def start_sends(slot):
        y_of = [(y + d) % 4 * 2 for d in range(4)]
        z_of = [(z + d) % 4 for d in range(4)]
        z_tm, z_rows = [v // 2 for v in z_of], [v % 2 * 8 for v in z_of]
        core_of = [core, 1 - core]

        @pl.loop(0, 4)
        def _(turn):
            x_of = [(x + 3 * turn + d) % 4 * 2 for d in range(4)]

            def start(step):
                shift = step * 91 % DEVICES
                to_tm = x_of[shift // 32] + z_tm[shift // 2 % 4]
                to_rows = z_rows[shift // 2 % 4] + y_of[shift // 8 % 4] + core_of[shift % 2]
                target = to_tm * ROWS + to_rows
                pltpu.make_async_remote_copy(
                    src_ref=send.at[slot, target // 4, target % 4],
                    dst_ref=recv.at[slot, me],
                    send_sem=send_sem.at[slot],
                    recv_sem=recv_sem.at[slot],
                    device_id={"tm": to_tm, "rows": to_rows},
                    device_id_type=MESH,
                ).start()

            @pl.when(turn > 0)
            def _():
                start(0)

            for step in range(1, 32):
                start(step)

        local_copy(slot).start()

    def local_copy(slot):
        return pltpu.make_async_copy(
            send.at[slot, me // 4, me % 4], recv.at[slot, me], local_sem.at[slot]
        )

    def wait_all(slot, sem):
        blocks = recv.at[slot, pl.ds(0, DEVICES - 1)]
        pltpu.make_async_copy(blocks, blocks, sem.at[slot]).wait()

    def gather_phase(slot):
        @pl.loop(0, TM)
        def _(block):
            low = lax.broadcasted_iota(jnp.int32, (16, 256), 1) % 128 < 64
            for pair in range(8):
                even = recv[slot, block * ROWS + 2 * pair]
                odd = recv[slot, block * ROWS + 2 * pair + 1]
                first = jnp.where(low, even, odd)
                second = jnp.where(low, odd, even)
                for inner in range(2):
                    at = pl.ds(pl.multiple_of(block * 32 + inner * 16, 16), 16)
                    lanes = slice(inner * 128, inner * 128 + 128)
                    columns = slice(pair * 128, pair * 128 + 128)
                    lhs[0, at, columns] = first[:, lanes]
                    lhs[1, at, columns] = second[:, lanes]

    def column_phase(part):
        columns = slice(part * 256, part * 256 + 256)
        above = slice(HALF + part * 256, HALF + part * 256 + 256)
        for second in range(2):
            table = txb if second else txa
            rc[...] = jnp.dot(lhs[second], table[:, columns], preferred_element_type=F32)
            rs[...] = jnp.dot(lhs[second], table[:, above], preferred_element_type=F32)

            @pl.loop(0, TM)
            def _(block):
                at = pl.ds(pl.multiple_of(block * 32, 32), 32)
                cosine = rc[at].reshape(4, 8, 256)
                sine = rs[at].reshape(4, 8, 256)
                top = lax.broadcasted_iota(jnp.int32, (4, 8, 256), 1) < 4
                swapped = pltpu.roll(sine, 4, 1)
                swapped = jnp.where(top, swapped, -swapped)
                plus, minus = cosine + swapped, cosine - swapped
                if part == 0:
                    edge = lax.broadcasted_iota(jnp.int32, (4, 8, 256), 2) == 0
                    plus = jnp.where(edge, cosine, plus)
                    minus = jnp.where(edge, sine, minus)
                modes[block, second, :, columns] = plus.reshape(32, 256).astype(BF16)
                modes[block, second, :, above] = minus.reshape(32, 256).astype(BF16)

    def window_at(window, columns):
        return modes[pl.ds(window, 2), :, :, columns].reshape(128, 256)

    def time_phase(slot, part):
        for half in range(2):
            columns = slice(half * HALF + part * 256, half * HALF + part * 256 + 256)
            total = None
            for window in range(TM - 1):
                u = jnp.dot(
                    time_ref[:128], window_at(window, columns), preferred_element_type=F32
                )
                u = u * u
                power = u[:64] + u[64:]
                total = power if total is None else total + power
            own_ref[slot, :, columns] = total
            msg[slot, part, :, half * 256 : half * 256 + 256] = total.astype(BF16)

        @pl.when((me == 0) & (slot == 0))
        def _():
            columns = slice(part * 256, part * 256 + 256)
            above = slice(HALF + part * 256, HALF + part * 256 + 256)
            lane = lax.broadcasted_iota(jnp.int32, (128, 256), 1) + part * 256
            sums = [None] * 4
            for window in range(TM - 1):
                a, b = (
                    jnp.dot(time_ref[...], window_at(window, at), preferred_element_type=F32)
                    for at in (columns, above)
                )
                back_a = jnp.where(lane == 0, a[128:], b[128:])
                back_b = jnp.where(lane == 0, b[128:], a[128:])
                terms = []
                for here, back in ((a[:128], back_a), (b[:128], back_b)):
                    r, i, rb, ib = here[:64], here[64:], back[:64], back[64:]
                    terms.append((r + rb) * (r + rb) + (i - ib) * (i - ib))
                    terms.append((r - rb) * (r - rb) + (i + ib) * (i + ib))
                sums = [t if s is None else s + t for s, t in zip(sums, terms)]
            own_ref[0, :, columns] = sums[0] * 0.25
            own_ref[0, :, above] = sums[2] * 0.25
            msg[0, part, :, :256] = (sums[1] * 0.25).astype(BF16)
            msg[0, part, :, 256:] = (sums[3] * 0.25).astype(BF16)

    def own_phase(slot):
        swap = (lax.broadcasted_iota(jnp.int32, (WIN, HALF), 1) >= 1) & (me >= 64)
        a, b = own_ref[slot, :, :HALF], own_ref[slot, :, HALF:]
        a, b = jnp.where(swap, b, a), jnp.where(swap, a, b)
        a_top, b_top = a.astype(BF16), b.astype(BF16)
        stack[slot, 0, :, :HALF] = a_top
        stack[slot, 1, :, :HALF] = (a - a_top.astype(F32)).astype(BF16)
        falling = jnp.concatenate([b_top, (b - b_top.astype(F32)).astype(BF16)], 0)
        falling = jnp.dot(falling, flip[...], preferred_element_type=F32).astype(BF16)
        stack[slot, 0, :, HALF:] = falling[:WIN]
        stack[slot, 1, :, HALF:] = falling[WIN:]

    def own_copy(slot):
        return pltpu.make_async_copy(stack.at[slot], own_hbm.at[slot], own_sem.at[slot])

    mirror = DEVICES - 1 - me
    first_to = jnp.where(me == 0, 64, jnp.where(me < 64, DEVICES - me, mirror))

    def message(slot, part):
        target = jnp.where(slot == 0, first_to, mirror)
        return pltpu.make_async_remote_copy(
            src_ref=msg.at[slot, part],
            dst_ref=got_hbm.at[slot, part],
            send_sem=msg_send_sem.at[slot, part],
            recv_sem=msg_recv_sem.at[slot, part],
            device_id={"tm": target // ROWS, "rows": target % ROWS},
            device_id_type=MESH,
        )

    loads[0].wait()
    row_tables(0)
    row_phase(0)
    pl.semaphore_wait(barrier, DEVICES - 1)
    loads[1].wait()
    for slot in range(1, SLOTS):
        row_tables(slot)

    @pl.loop(0, SLOTS)
    def _(slot):
        start_sends(slot)

        @pl.when(slot < SLOTS - 1)
        def _():
            row_phase(slot + 1)

    loads[2].wait()
    column_tables()
    make_flip(flip)

    @pl.loop(0, SLOTS)
    def _(slot):
        local_copy(slot).wait()
        wait_all(slot, recv_sem)
        gather_phase(slot)
        for part in range(2):
            column_phase(part)
            time_phase(slot, part)
            message(slot, part).start()
        own_phase(slot)
        own_copy(slot).start()

    @pl.loop(0, SLOTS)
    def _(slot):
        wait_all(slot, send_sem)
        own_copy(slot).wait()
        for part in range(2):
            message(slot, part).wait()


def final_kernel(
    scale, own_hbm, got_hbm, out_hbm, stack, got_ref, left, flip, result, in_sem, out_sem
):
    loads = [
        pltpu.make_async_copy(got_hbm, got_ref, in_sem.at[0]),
        pltpu.make_async_copy(own_hbm, stack.at[pl.ds(0, HALF)], in_sem.at[1]),
    ]
    for load in loads:
        load.start()
    me = lax.axis_index("tm") * ROWS + lax.axis_index("rows")
    upper = me >= 64
    make_flip(flip)
    to = lax.broadcasted_iota(jnp.int32, (HALF, HALF), 0)
    come = lax.broadcasted_iota(jnp.int32, (HALF, HALF), 1)
    w, row = to // 8, to % 8
    w_from = jnp.where(upper, (WIN - w) % WIN, w)
    slot_own = jnp.where(
        upper, jnp.where((row >= 1) & (row <= 4), 4 - row, -1), jnp.where(row < 4, row, -1)
    )
    slot_got = jnp.where(
        upper,
        jnp.where(row == 0, 0, jnp.where(row >= 5, 8 - row, -1)),
        jnp.where(row >= 4, row - 4, -1),
    )
    from_own = (come // 128 == slot_own) & (come % WIN == w_from)
    from_got = come == slot_got * WIN + w_from
    left[:, :HALF] = jnp.where(from_own, 1.0, 0.0).astype(BF16)
    left[:, HALF:] = jnp.where(from_got, 1.0, 0.0)[:, :256].astype(BF16)
    swap = (lax.broadcasted_iota(jnp.int32, (256, HALF), 1) >= 1) & upper

    loads[0].wait()
    a, b = (
        jnp.concatenate(
            [got_ref[:, part, :, at].reshape(256, 256).astype(F32) for part in range(2)], 1
        )
        for at in (slice(0, 256), slice(256, 512))
    )
    stack[HALF:, :HALF] = jnp.where(swap, b, a).astype(BF16)
    falling = jnp.where(swap, a, b).astype(BF16)
    falling = jnp.dot(falling, flip[...], preferred_element_type=F32).astype(BF16)
    stack[HALF:, HALF:] = falling
    loads[1].wait()

    stores = []
    for part in range(4):
        columns = slice(part * 256, part * 256 + 256)
        product = jnp.dot(left[...], stack[:, columns], preferred_element_type=F32) * scale
        result[part] = product.reshape(WIN, 8, 256)
        store = pltpu.make_async_copy(
            result.at[part], out_hbm.at[:, :, pl.ds(part * 256, 256)], out_sem.at[part]
        )
        store.start()
        stores.append(store)
    for store in stores:
        store.wait()


def body(heights):
    vmem = pl.BlockSpec(memory_space=pltpu.VMEM)
    hbm = pl.BlockSpec(memory_space=pl.ANY)
    energy = tapers()[2]
    dma = pltpu.SemaphoreType.DMA
    own, got = pl.pallas_call(
        spectrum_kernel,
        out_shape=(
            jax.ShapeDtypeStruct((SLOTS, 2, WIN, GRID), BF16),
            jax.ShapeDtypeStruct((SLOTS, 2, WIN, HALF), BF16),
        ),
        in_specs=[hbm] * 3 + [vmem],
        out_specs=(hbm, hbm),
        scratch_shapes=[
            pltpu.VMEM((FRAMES_DEV, X_DEV, GRID), BF16),
            pltpu.VMEM((SLOTS, QUARTER, HALF), BF16),
            pltpu.VMEM((HALF, GRID), BF16),
            pltpu.VMEM((SLOTS, WIN, GRID), F32),
            pltpu.VMEM((SLOTS, QUARTER, GRID), BF16),
            pltpu.VMEM((GRID, GRID), BF16),
            pltpu.VMEM((GRID, GRID), BF16),
            pltpu.VMEM((8, QUARTER, 256), F32),
            pltpu.VMEM((SLOTS, DEVICES // 4, 4, 16, 256), BF16),
            pltpu.VMEM((SLOTS, DEVICES, 16, 256), BF16),
            pltpu.VMEM((2, QUARTER, GRID), BF16),
            pltpu.VMEM((QUARTER, 256), F32),
            pltpu.VMEM((QUARTER, 256), F32),
            pltpu.VMEM((TM, 2, 32, GRID), BF16),
            pltpu.VMEM((SLOTS, 2, WIN, HALF), BF16),
            pltpu.VMEM((SLOTS, 2, WIN, GRID), BF16),
            pltpu.VMEM((HALF, HALF), BF16),
            dma((SLOTS,)),
            dma((SLOTS,)),
            dma((SLOTS,)),
            dma((SLOTS, 2)),
            dma((SLOTS, 2)),
            dma((3,)),
            dma((8,)),
            dma((SLOTS,)),
        ],
        compiler_params=pltpu.CompilerParams(
            collective_id=0, has_side_effects=True, vmem_limit_bytes=VMEM_ALL
        ),
    )(
        heights,
        jnp.asarray(row_table()),
        jnp.asarray(column_table()),
        jnp.asarray(time_matrices()),
    )
    return pl.pallas_call(
        functools.partial(final_kernel, 1.0 / ((TM - 1) * energy)),
        out_shape=jax.ShapeDtypeStruct((WIN, 8, GRID), F32),
        in_specs=[hbm, hbm],
        out_specs=hbm,
        scratch_shapes=[
            pltpu.VMEM((768, GRID), BF16),
            pltpu.VMEM((SLOTS, 2, WIN, HALF), BF16),
            pltpu.VMEM((HALF, 768), BF16),
            pltpu.VMEM((HALF, HALF), BF16),
            pltpu.VMEM((4, WIN, 8, 256), F32),
            dma((2,)),
            dma((4,)),
        ],
        compiler_params=pltpu.CompilerParams(vmem_limit_bytes=VMEM_ALL),
    )(own.reshape(HALF, GRID), got)


def solution(mesh):
    return jax.shard_map(
        body,
        mesh=mesh,
        in_specs=(P("tm", "rows", None),),
        out_specs=P(None, ("tm", "rows"), None),
        check_vma=False,
    )
```

```python
import functools
import math

import jax
import jax.numpy as jnp
import ml_dtypes
import numpy as np
from jax import lax
from jax.experimental import pallas as pl
from jax.experimental.pallas import tpu as pltpu
from jax.sharding import PartitionSpec as P

MESH = pl.DeviceIdType.MESH
GRID = 1024
HALF = 512
WIN = 64
TM = 8
ROWS = 16
DEVICES = TM * ROWS
FRAMES_DEV = 32
X_DEV = 64
SLOTS = 4
QUARTER = 256
VMEM_ALL = 67_000_000
BF16 = jnp.bfloat16
F32 = jnp.float32


def trig(index):
    angles = (index % GRID).astype(np.float32) * np.float32(2.0 * math.pi / GRID)
    scale = np.float32(math.sqrt(GRID))
    return np.cos(angles) / scale, np.sin(angles) / scale


def row_table():
    row = np.arange(QUARTER)
    quad, part, low = row // 8, row // 4 % 2, row % 4
    device = 4 * quad + low
    y = np.arange(HALF)
    tables = []
    for slot in range(SLOTS):
        q = np.where(device < 64, 8 * device + slot, 8 * (127 - device) + 4 + slot)
        cosine, sine = trig(q[:, None] * y[None, :])
        values = np.where(part[:, None] == 0, cosine, -sine)
        shared = (device == 0) & (slot == 0) & (part == 1)
        nyquist, _ = trig(HALF * y)
        tables.append(np.where(shared[:, None], nyquist[None, :], values))
    return np.stack(tables).astype(ml_dtypes.bfloat16)


def column_table():
    x = np.arange(HALF)
    cosine, sine = trig(x[:, None] * x[None, :])
    sine[:, 0] = trig(x * HALF)[0]
    return np.concatenate([cosine, sine], 1).astype(ml_dtypes.bfloat16)


def tapers():
    t = np.arange(WIN)
    hann = np.float32(0.5) - np.float32(0.5) * np.cos(
        t.astype(np.float32) * np.float32(2.0 * math.pi / WIN)
    )
    angles = (t[:, None] * t[None, :] % WIN).astype(np.float32) * np.float32(2.0 * math.pi / WIN)
    energy = float(np.sum(hann * hann, dtype=np.float32))

    def rounded(values):
        return (values * hann[None, :]).astype(ml_dtypes.bfloat16).astype(np.float32)

    return rounded(np.cos(angles)), rounded(np.sin(angles)), energy


def time_matrices():
    cosine, sine, _ = tapers()
    k = np.arange(128)
    block, second, inner = k // 64, k // 32 % 2, k // 16 % 2
    high, part, low = k // 8 % 2, k // 4 % 2, k % 4
    t = 32 * block + 16 * high + 4 * low + 2 * inner + second
    real = np.where(part == 0, cosine[:, t], sine[:, t])
    imag = np.where(part == 0, -sine[:, t], cosine[:, t])
    back = (-np.arange(WIN)) % WIN
    return np.concatenate([real, imag, real[back], imag[back]]).astype(ml_dtypes.bfloat16)


def far(step):
    a, b = step // ROWS, step % ROWS
    return min(a // 2, 4 - a // 2) + a % 2 * 2 + b // 8 + min(b // 2 % 4, 4 - b // 2 % 4)


def make_flip(flip):
    i = lax.broadcasted_iota(jnp.int32, (HALF, HALF), 0)
    j = lax.broadcasted_iota(jnp.int32, (HALF, HALF), 1)
    flip[...] = jnp.where(i == (HALF - j) % HALF, 1.0, 0.0).astype(BF16)


def spectrum_kernel(
    h_hbm, ty_hbm, tx_hbm, time_ref, own_hbm, got_hbm,
    h_ref, ty_ref, tx_ref, own_ref, tab, txa, txb, rowsum, send, recv, lhs, rc, rs, modes, msg, stack, flip,
    send_sem, recv_sem, local_sem, msg_send_sem, msg_recv_sem, load_sem, height_sem, own_sem,
):
    tm, rows = lax.axis_index("tm"), lax.axis_index("rows")
    me = tm * ROWS + rows
    x, y, z, core = tm // 2, rows // 2 % 4, tm % 2 * 2 + rows // 8, rows % 2

    def height_load(eighth):
        frames = pl.ds(eighth * 4, 4)
        return pltpu.make_async_copy(h_hbm.at[frames], h_ref.at[frames], height_sem.at[eighth])

    later = pl.ds(1, SLOTS - 1)
    loads = [
        pltpu.make_async_copy(ty_hbm.at[0], ty_ref.at[0], load_sem.at[0]),
        pltpu.make_async_copy(ty_hbm.at[later], ty_ref.at[later], load_sem.at[1]),
        pltpu.make_async_copy(tx_hbm, tx_ref, load_sem.at[2]),
    ]
    loads[0].start()
    for eighth in range(8):
        height_load(eighth).start()
    loads[1].start()
    loads[2].start()

    barrier = pltpu.get_barrier_semaphore()
    tm_of = [(tm + a) % TM for a in range(TM)]
    rows_of = [(rows + b) % ROWS for b in range(ROWS)]
    for step in sorted(range(1, DEVICES), key=far, reverse=True):
        pl.semaphore_signal(
            barrier,
            inc=1,
            device_id={"tm": tm_of[step // ROWS], "rows": rows_of[step % ROWS]},
            device_id_type=MESH,
        )

    def row_tables(slot):
        tab[slot, :, :HALF] = ty_ref[slot]
        tab[slot, :, HALF:] = -ty_ref[slot] if slot % 2 else ty_ref[slot]

    def column_tables():
        lane_sign = jnp.where(lax.broadcasted_iota(jnp.int32, (1, GRID), 1) % 2 == 0, 1.0, -1.0)
        txa[:HALF] = tx_ref[...]
        txa[HALF:] = (tx_ref[...].astype(F32) * lane_sign).astype(BF16)

        @pl.loop(0, 8)
        def _(block):
            base = pl.multiple_of(block * 128, 128)
            txb[pl.ds(base, 64)] = txa[pl.ds(base + 64, 64)]
            txb[pl.ds(base + 64, 64)] = txa[pl.ds(base, 64)]

    def row_phase(slot):
        first = isinstance(slot, int)

        @pl.loop(0, 8)
        def _(eighth):
            if first:
                height_load(eighth).wait()
            base = eighth * 4
            block = jnp.concatenate(
                [
                    h_ref[base + core],
                    h_ref[base + 1 - core],
                    h_ref[base + 2 + core],
                    h_ref[base + 3 - core],
                ],
                0,
            )
            rowsum[eighth] = lax.dot_general(
                tab[slot], block, (((1,), (1,)), ((), ())), preferred_element_type=F32
            )

        @pl.loop(0, 8)
        def _(part):
            at = pl.ds(pl.multiple_of(part * 32, 32), 32)
            row = lax.broadcasted_iota(jnp.int32, (4, 8, 256), 1)
            pair, single = row // 2 % 2 == 0, row % 2 == 0
            halves = []
            for high in range(2):
                r = [rowsum[4 * high + f, at].reshape(4, 8, 256) for f in range(4)]
                a = [None] * 4
                for f in range(2):
                    a[f] = jnp.where(pair, r[f], pltpu.roll(r[f + 2], 2, 1))
                    a[f + 2] = jnp.where(pair, pltpu.roll(r[f], 6, 1), r[f + 2])
                halves.append(
                    [
                        jnp.where(single, a[0], pltpu.roll(a[1], 1, 1)),
                        jnp.where(single, pltpu.roll(a[0], 7, 1), a[1]),
                        jnp.where(single, a[2], pltpu.roll(a[3], 1, 1)),
                        jnp.where(single, pltpu.roll(a[2], 7, 1), a[3]),
                    ]
                )
            for low in range(4):
                send[slot, pl.ds(part * 4, 4), low] = jnp.concatenate(
                    [halves[0][low], halves[1][low]], 1
                ).astype(BF16)

    def start_sends(slot):
        y_of = [(y + d) % 4 * 2 for d in range(4)]
        z_of = [(z + d) % 4 for d in range(4)]
        z_tm, z_rows = [v // 2 for v in z_of], [v % 2 * 8 for v in z_of]
        core_of = [core, 1 - core]

        @pl.loop(0, 4)
        def _(turn):
            x_of = [(x + 3 * turn + d) % 4 * 2 for d in range(4)]

            def start(step):
                shift = step * 91 % DEVICES
                to_tm = x_of[shift // 32] + z_tm[shift // 2 % 4]
                to_rows = z_rows[shift // 2 % 4] + y_of[shift // 8 % 4] + core_of[shift % 2]
                target = to_tm * ROWS + to_rows
                pltpu.make_async_remote_copy(
                    src_ref=send.at[slot, target // 4, target % 4],
                    dst_ref=recv.at[slot, me],
                    send_sem=send_sem.at[slot],
                    recv_sem=recv_sem.at[slot],
                    device_id={"tm": to_tm, "rows": to_rows},
                    device_id_type=MESH,
                ).start()

            @pl.when(turn > 0)
            def _():
                start(0)

            for step in range(1, 32):
                start(step)

        local_copy(slot).start()

    def local_copy(slot):
        return pltpu.make_async_copy(
            send.at[slot, me // 4, me % 4], recv.at[slot, me], local_sem.at[slot]
        )

    def wait_all(slot, sem):
        blocks = recv.at[slot, pl.ds(0, DEVICES - 1)]
        pltpu.make_async_copy(blocks, blocks, sem.at[slot]).wait()

    def gather_phase(slot):
        @pl.loop(0, TM)
        def _(block):
            low = lax.broadcasted_iota(jnp.int32, (16, 256), 1) % 128 < 64
            for pair in range(8):
                even = recv[slot, block * ROWS + 2 * pair]
                odd = recv[slot, block * ROWS + 2 * pair + 1]
                first = jnp.where(low, even, odd)
                second = jnp.where(low, odd, even)
                for inner in range(2):
                    at = pl.ds(pl.multiple_of(block * 32 + inner * 16, 16), 16)
                    lanes = slice(inner * 128, inner * 128 + 128)
                    columns = slice(pair * 128, pair * 128 + 128)
                    lhs[0, at, columns] = first[:, lanes]
                    lhs[1, at, columns] = second[:, lanes]

    def column_phase(part):
        columns = slice(part * 256, part * 256 + 256)
        above = slice(HALF + part * 256, HALF + part * 256 + 256)
        for second in range(2):
            table = txb if second else txa
            rc[...] = jnp.dot(lhs[second], table[:, columns], preferred_element_type=F32)
            rs[...] = jnp.dot(lhs[second], table[:, above], preferred_element_type=F32)

            @pl.loop(0, TM)
            def _(block):
                at = pl.ds(pl.multiple_of(block * 32, 32), 32)
                cosine = rc[at].reshape(4, 8, 256)
                sine = rs[at].reshape(4, 8, 256)
                top = lax.broadcasted_iota(jnp.int32, (4, 8, 256), 1) < 4
                swapped = pltpu.roll(sine, 4, 1)
                swapped = jnp.where(top, swapped, -swapped)
                plus, minus = cosine + swapped, cosine - swapped
                if part == 0:
                    edge = lax.broadcasted_iota(jnp.int32, (4, 8, 256), 2) == 0
                    plus = jnp.where(edge, cosine, plus)
                    minus = jnp.where(edge, sine, minus)
                modes[block, second, :, columns] = plus.reshape(32, 256).astype(BF16)
                modes[block, second, :, above] = minus.reshape(32, 256).astype(BF16)

    def window_at(window, columns):
        return modes[pl.ds(window, 2), :, :, columns].reshape(128, 256)

    def time_phase(slot, part):
        for half in range(2):
            columns = slice(half * HALF + part * 256, half * HALF + part * 256 + 256)
            total = None
            for window in range(TM - 1):
                u = jnp.dot(
                    time_ref[:128], window_at(window, columns), preferred_element_type=F32
                )
                u = u * u
                power = u[:64] + u[64:]
                total = power if total is None else total + power
            own_ref[slot, :, columns] = total
            msg[slot, part, :, half * 256 : half * 256 + 256] = total.astype(BF16)

        @pl.when((me == 0) & (slot == 0))
        def _():
            columns = slice(part * 256, part * 256 + 256)
            above = slice(HALF + part * 256, HALF + part * 256 + 256)
            lane = lax.broadcasted_iota(jnp.int32, (128, 256), 1) + part * 256
            sums = [None] * 4
            for window in range(TM - 1):
                a, b = (
                    jnp.dot(time_ref[...], window_at(window, at), preferred_element_type=F32)
                    for at in (columns, above)
                )
                back_a = jnp.where(lane == 0, a[128:], b[128:])
                back_b = jnp.where(lane == 0, b[128:], a[128:])
                terms = []
                for here, back in ((a[:128], back_a), (b[:128], back_b)):
                    r, i, rb, ib = here[:64], here[64:], back[:64], back[64:]
                    terms.append((r + rb) * (r + rb) + (i - ib) * (i - ib))
                    terms.append((r - rb) * (r - rb) + (i + ib) * (i + ib))
                sums = [t if s is None else s + t for s, t in zip(sums, terms)]
            own_ref[0, :, columns] = sums[0] * 0.25
            own_ref[0, :, above] = sums[2] * 0.25
            msg[0, part, :, :256] = (sums[1] * 0.25).astype(BF16)
            msg[0, part, :, 256:] = (sums[3] * 0.25).astype(BF16)

    def own_phase(slot):
        swap = (lax.broadcasted_iota(jnp.int32, (WIN, HALF), 1) >= 1) & (me >= 64)
        a, b = own_ref[slot, :, :HALF], own_ref[slot, :, HALF:]
        a, b = jnp.where(swap, b, a), jnp.where(swap, a, b)
        falling = jnp.dot(b.astype(BF16), flip[...], preferred_element_type=F32)
        stack[slot, :, :HALF] = a.astype(BF16)
        stack[slot, :, HALF:] = falling.astype(BF16)

    def own_copy(slot):
        return pltpu.make_async_copy(stack.at[slot], own_hbm.at[slot], own_sem.at[slot])

    mirror = DEVICES - 1 - me
    first_to = jnp.where(me == 0, 64, jnp.where(me < 64, DEVICES - me, mirror))

    def message(slot, part):
        target = jnp.where(slot == 0, first_to, mirror)
        return pltpu.make_async_remote_copy(
            src_ref=msg.at[slot, part],
            dst_ref=got_hbm.at[slot, part],
            send_sem=msg_send_sem.at[slot, part],
            recv_sem=msg_recv_sem.at[slot, part],
            device_id={"tm": target // ROWS, "rows": target % ROWS},
            device_id_type=MESH,
        )

    loads[0].wait()
    row_tables(0)
    row_phase(0)
    pl.semaphore_wait(barrier, DEVICES - 1)
    loads[1].wait()
    for slot in range(1, SLOTS):
        row_tables(slot)

    @pl.loop(0, SLOTS)
    def _(slot):
        start_sends(slot)

        @pl.when(slot < SLOTS - 1)
        def _():
            row_phase(slot + 1)

    loads[2].wait()
    column_tables()
    make_flip(flip)

    @pl.loop(0, SLOTS)
    def _(slot):
        local_copy(slot).wait()
        wait_all(slot, recv_sem)
        gather_phase(slot)
        for part in range(2):
            column_phase(part)
            time_phase(slot, part)
            message(slot, part).start()
        own_phase(slot)
        own_copy(slot).start()

    @pl.loop(0, SLOTS)
    def _(slot):
        wait_all(slot, send_sem)
        own_copy(slot).wait()
        for part in range(2):
            message(slot, part).wait()


def final_kernel(
    scale, own_hbm, got_hbm, out_hbm, stack, got_ref, left, flip, result, in_sem, out_sem
):
    loads = [pltpu.make_async_copy(got_hbm, got_ref, in_sem.at[0])]
    for half in range(2):
        columns = pl.ds(half * HALF, HALF)
        loads.append(
            pltpu.make_async_copy(
                own_hbm.at[:, columns], stack.at[pl.ds(0, 256), columns], in_sem.at[1 + half]
            )
        )
    for load in loads:
        load.start()
    me = lax.axis_index("tm") * ROWS + lax.axis_index("rows")
    upper = me >= 64
    make_flip(flip)
    to = lax.broadcasted_iota(jnp.int32, (HALF, HALF), 0)
    come = lax.broadcasted_iota(jnp.int32, (HALF, HALF), 1)
    w, row = to // 8, to % 8
    mirrored = jnp.where(row == 0, 4, jnp.where(row <= 4, 4 - row, 12 - row))
    source = jnp.where(upper, mirrored * WIN + (WIN - w) % WIN, row * WIN + w)
    left[...] = jnp.where(come == source, 1.0, 0.0).astype(BF16)
    swap = (lax.broadcasted_iota(jnp.int32, (256, HALF), 1) >= 1) & upper

    stores = []

    def place(part):
        columns = slice(part * 256, part * 256 + 256)
        product = jnp.dot(left[...], stack[:, columns], preferred_element_type=F32) * scale
        result[part] = product.reshape(WIN, 8, 256)
        store = pltpu.make_async_copy(
            result.at[part], out_hbm.at[:, :, pl.ds(part * 256, 256)], out_sem.at[part]
        )
        store.start()
        stores.append(store)

    loads[0].wait()
    a, b = (
        jnp.concatenate(
            [got_ref[:, part, :, at].reshape(256, 256).astype(F32) for part in range(2)], 1
        )
        for at in (slice(0, 256), slice(256, 512))
    )
    stack[256:, :HALF] = jnp.where(swap, b, a).astype(BF16)
    loads[1].wait()
    place(0)
    place(1)
    falling = jnp.where(swap, a, b).astype(BF16)
    falling = jnp.dot(falling, flip[...], preferred_element_type=F32)
    stack[256:, HALF:] = falling.astype(BF16)
    loads[2].wait()
    place(2)
    place(3)
    for store in stores:
        store.wait()


def body(heights):
    vmem = pl.BlockSpec(memory_space=pltpu.VMEM)
    hbm = pl.BlockSpec(memory_space=pl.ANY)
    energy = tapers()[2]
    dma = pltpu.SemaphoreType.DMA
    own, got = pl.pallas_call(
        spectrum_kernel,
        out_shape=(
            jax.ShapeDtypeStruct((SLOTS, WIN, GRID), BF16),
            jax.ShapeDtypeStruct((SLOTS, 2, WIN, HALF), BF16),
        ),
        in_specs=[hbm] * 3 + [vmem],
        out_specs=(hbm, hbm),
        scratch_shapes=[
            pltpu.VMEM((FRAMES_DEV, X_DEV, GRID), BF16),
            pltpu.VMEM((SLOTS, QUARTER, HALF), BF16),
            pltpu.VMEM((HALF, GRID), BF16),
            pltpu.VMEM((SLOTS, WIN, GRID), F32),
            pltpu.VMEM((SLOTS, QUARTER, GRID), BF16),
            pltpu.VMEM((GRID, GRID), BF16),
            pltpu.VMEM((GRID, GRID), BF16),
            pltpu.VMEM((8, QUARTER, 256), F32),
            pltpu.VMEM((SLOTS, DEVICES // 4, 4, 16, 256), BF16),
            pltpu.VMEM((SLOTS, DEVICES, 16, 256), BF16),
            pltpu.VMEM((2, QUARTER, GRID), BF16),
            pltpu.VMEM((QUARTER, 256), F32),
            pltpu.VMEM((QUARTER, 256), F32),
            pltpu.VMEM((TM, 2, 32, GRID), BF16),
            pltpu.VMEM((SLOTS, 2, WIN, HALF), BF16),
            pltpu.VMEM((SLOTS, WIN, GRID), BF16),
            pltpu.VMEM((HALF, HALF), BF16),
            dma((SLOTS,)),
            dma((SLOTS,)),
            dma((SLOTS,)),
            dma((SLOTS, 2)),
            dma((SLOTS, 2)),
            dma((3,)),
            dma((8,)),
            dma((SLOTS,)),
        ],
        compiler_params=pltpu.CompilerParams(
            collective_id=0, has_side_effects=True, vmem_limit_bytes=VMEM_ALL
        ),
    )(
        heights,
        jnp.asarray(row_table()),
        jnp.asarray(column_table()),
        jnp.asarray(time_matrices()),
    )
    return pl.pallas_call(
        functools.partial(final_kernel, 1.0 / ((TM - 1) * energy)),
        out_shape=jax.ShapeDtypeStruct((WIN, 8, GRID), F32),
        in_specs=[hbm, hbm],
        out_specs=hbm,
        scratch_shapes=[
            pltpu.VMEM((HALF, GRID), BF16),
            pltpu.VMEM((SLOTS, 2, WIN, HALF), BF16),
            pltpu.VMEM((HALF, HALF), BF16),
            pltpu.VMEM((HALF, HALF), BF16),
            pltpu.VMEM((4, WIN, 8, 256), F32),
            dma((3,)),
            dma((4,)),
        ],
        compiler_params=pltpu.CompilerParams(vmem_limit_bytes=VMEM_ALL),
    )(own.reshape(256, GRID), got)


def solution(mesh):
    return jax.shard_map(
        body,
        mesh=mesh,
        in_specs=(P("tm", "rows", None),),
        out_specs=P(None, ("tm", "rows"), None),
        check_vma=False,
    )
```

```python
import functools
import math

import jax
import jax.numpy as jnp
import ml_dtypes
import numpy as np
from jax import lax
from jax.experimental import pallas as pl
from jax.experimental.pallas import tpu as pltpu
from jax.sharding import PartitionSpec as P

MESH = pl.DeviceIdType.MESH
GRID = 1024
HALF = 512
WIN = 64
TM = 8
ROWS = 16
DEVICES = TM * ROWS
FRAMES_DEV = 32
X_DEV = 64
SLOTS = 4
QUARTER = 256
VMEM_ALL = 67_000_000
BF16 = jnp.bfloat16
F32 = jnp.float32


def trig(index):
    angles = (index % GRID).astype(np.float32) * np.float32(2.0 * math.pi / GRID)
    scale = np.float32(math.sqrt(GRID))
    return np.cos(angles) / scale, np.sin(angles) / scale


def row_table():
    row = np.arange(QUARTER)
    quad, part, low = row // 8, row // 4 % 2, row % 4
    device = 4 * quad + low
    y = np.arange(HALF)
    tables = []
    for slot in range(SLOTS):
        q = np.where(device < 64, 8 * device + slot, 8 * (127 - device) + 4 + slot)
        cosine, sine = trig(q[:, None] * y[None, :])
        values = np.where(part[:, None] == 0, cosine, -sine)
        shared = (device == 0) & (slot == 0) & (part == 1)
        nyquist, _ = trig(HALF * y)
        tables.append(np.where(shared[:, None], nyquist[None, :], values))
    return np.stack(tables).astype(ml_dtypes.bfloat16)


def column_table():
    x = np.arange(HALF)
    cosine, sine = trig(x[:, None] * x[None, :])
    sine[:, 0] = trig(x * HALF)[0]
    return np.concatenate([cosine, sine], 1).astype(ml_dtypes.bfloat16)


def tapers():
    t = np.arange(WIN)
    hann = np.float32(0.5) - np.float32(0.5) * np.cos(
        t.astype(np.float32) * np.float32(2.0 * math.pi / WIN)
    )
    angles = (t[:, None] * t[None, :] % WIN).astype(np.float32) * np.float32(2.0 * math.pi / WIN)
    energy = float(np.sum(hann * hann, dtype=np.float32))

    def rounded(values):
        return (values * hann[None, :]).astype(ml_dtypes.bfloat16).astype(np.float32)

    return rounded(np.cos(angles)), rounded(np.sin(angles)), energy


def time_matrices():
    cosine, sine, _ = tapers()
    k = np.arange(128)
    block, second, inner = k // 64, k // 32 % 2, k // 16 % 2
    high, part, low = k // 8 % 2, k // 4 % 2, k % 4
    t = 32 * block + 16 * high + 4 * low + 2 * inner + second
    real = np.where(part == 0, cosine[:, t], sine[:, t])
    imag = np.where(part == 0, -sine[:, t], cosine[:, t])
    back = (-np.arange(WIN)) % WIN
    return np.concatenate([real, imag, real[back], imag[back]]).astype(ml_dtypes.bfloat16)


def far(step):
    a, b = step // ROWS, step % ROWS
    return min(a // 2, 4 - a // 2) + a % 2 * 2 + b // 8 + min(b // 2 % 4, 4 - b // 2 % 4)


def make_flip(flip):
    i = lax.broadcasted_iota(jnp.int32, (HALF, HALF), 0)
    j = lax.broadcasted_iota(jnp.int32, (HALF, HALF), 1)
    flip[...] = jnp.where(i == (HALF - j) % HALF, 1.0, 0.0).astype(BF16)


def spectrum_kernel(
    h_hbm, ty_hbm, tx_hbm, time_ref, own_hbm, got_hbm,
    h_ref, ty_ref, tx_ref, own_ref, tab, txa, txb, rowsum, send, recv, lhs, rc, rs, modes, msg, stack, flip,
    send_sem, recv_sem, local_sem, msg_send_sem, msg_recv_sem, load_sem, height_sem, own_sem,
):
    tm, rows = lax.axis_index("tm"), lax.axis_index("rows")
    me = tm * ROWS + rows
    x, y, z, core = tm // 2, rows // 2 % 4, tm % 2 * 2 + rows // 8, rows % 2

    def height_load(eighth):
        frames = pl.ds(eighth * 4, 4)
        return pltpu.make_async_copy(h_hbm.at[frames], h_ref.at[frames], height_sem.at[eighth])

    later = pl.ds(1, SLOTS - 1)
    loads = [
        pltpu.make_async_copy(ty_hbm.at[0], ty_ref.at[0], load_sem.at[0]),
        pltpu.make_async_copy(ty_hbm.at[later], ty_ref.at[later], load_sem.at[1]),
        pltpu.make_async_copy(tx_hbm, tx_ref, load_sem.at[2]),
    ]
    loads[0].start()
    for eighth in range(8):
        height_load(eighth).start()
    loads[1].start()
    loads[2].start()

    barrier = pltpu.get_barrier_semaphore()
    tm_of = [(tm + a) % TM for a in range(TM)]
    rows_of = [(rows + b) % ROWS for b in range(ROWS)]
    for step in sorted(range(1, DEVICES), key=far, reverse=True):
        pl.semaphore_signal(
            barrier,
            inc=1,
            device_id={"tm": tm_of[step // ROWS], "rows": rows_of[step % ROWS]},
            device_id_type=MESH,
        )

    def row_tables(slot):
        tab[slot, :, :HALF] = ty_ref[slot]
        tab[slot, :, HALF:] = -ty_ref[slot] if slot % 2 else ty_ref[slot]

    def column_tables():
        lane_sign = jnp.where(lax.broadcasted_iota(jnp.int32, (1, GRID), 1) % 2 == 0, 1.0, -1.0)
        txa[:HALF] = tx_ref[...]
        txa[HALF:] = (tx_ref[...].astype(F32) * lane_sign).astype(BF16)

        @pl.loop(0, 8)
        def _(block):
            base = pl.multiple_of(block * 128, 128)
            txb[pl.ds(base, 64)] = txa[pl.ds(base + 64, 64)]
            txb[pl.ds(base + 64, 64)] = txa[pl.ds(base, 64)]

    def row_phase(slot):
        first = isinstance(slot, int)

        @pl.loop(0, 8)
        def _(eighth):
            if first:
                height_load(eighth).wait()
            base = eighth * 4
            block = jnp.concatenate(
                [
                    h_ref[base + core],
                    h_ref[base + 1 - core],
                    h_ref[base + 2 + core],
                    h_ref[base + 3 - core],
                ],
                0,
            )
            rowsum[eighth] = lax.dot_general(
                tab[slot], block, (((1,), (1,)), ((), ())), preferred_element_type=F32
            )

        @pl.loop(0, 8)
        def _(part):
            at = pl.ds(pl.multiple_of(part * 32, 32), 32)
            row = lax.broadcasted_iota(jnp.int32, (4, 8, 256), 1)
            pair, single = row // 2 % 2 == 0, row % 2 == 0
            halves = []
            for high in range(2):
                r = [rowsum[4 * high + f, at].reshape(4, 8, 256) for f in range(4)]
                a = [None] * 4
                for f in range(2):
                    a[f] = jnp.where(pair, r[f], pltpu.roll(r[f + 2], 2, 1))
                    a[f + 2] = jnp.where(pair, pltpu.roll(r[f], 6, 1), r[f + 2])
                halves.append(
                    [
                        jnp.where(single, a[0], pltpu.roll(a[1], 1, 1)),
                        jnp.where(single, pltpu.roll(a[0], 7, 1), a[1]),
                        jnp.where(single, a[2], pltpu.roll(a[3], 1, 1)),
                        jnp.where(single, pltpu.roll(a[2], 7, 1), a[3]),
                    ]
                )
            for low in range(4):
                send[slot, pl.ds(part * 4, 4), low] = jnp.concatenate(
                    [halves[0][low], halves[1][low]], 1
                ).astype(BF16)

    def start_sends(slot):
        y_of = [(y + d) % 4 * 2 for d in range(4)]
        z_of = [(z + d) % 4 for d in range(4)]
        z_tm, z_rows = [v // 2 for v in z_of], [v % 2 * 8 for v in z_of]
        core_of = [core, 1 - core]

        @pl.loop(0, 4)
        def _(turn):
            x_of = [(x + 3 * turn + d) % 4 * 2 for d in range(4)]

            def start(step):
                shift = step * 91 % DEVICES
                to_tm = x_of[shift // 32] + z_tm[shift // 2 % 4]
                to_rows = z_rows[shift // 2 % 4] + y_of[shift // 8 % 4] + core_of[shift % 2]
                target = to_tm * ROWS + to_rows
                pltpu.make_async_remote_copy(
                    src_ref=send.at[slot, target // 4, target % 4],
                    dst_ref=recv.at[slot, me],
                    send_sem=send_sem.at[slot],
                    recv_sem=recv_sem.at[slot],
                    device_id={"tm": to_tm, "rows": to_rows},
                    device_id_type=MESH,
                ).start()

            @pl.when(turn > 0)
            def _():
                start(0)

            for step in range(1, 32):
                start(step)

        local_copy(slot).start()

    def local_copy(slot):
        return pltpu.make_async_copy(
            send.at[slot, me // 4, me % 4], recv.at[slot, me], local_sem.at[slot]
        )

    def wait_all(slot, sem):
        blocks = recv.at[slot, pl.ds(0, DEVICES - 1)]
        pltpu.make_async_copy(blocks, blocks, sem.at[slot]).wait()

    def gather_phase(slot):
        @pl.loop(0, TM)
        def _(block):
            low = lax.broadcasted_iota(jnp.int32, (16, 256), 1) % 128 < 64
            for pair in range(8):
                even = recv[slot, block * ROWS + 2 * pair]
                odd = recv[slot, block * ROWS + 2 * pair + 1]
                first = jnp.where(low, even, odd)
                second = jnp.where(low, odd, even)
                for inner in range(2):
                    at = pl.ds(pl.multiple_of(block * 32 + inner * 16, 16), 16)
                    lanes = slice(inner * 128, inner * 128 + 128)
                    columns = slice(pair * 128, pair * 128 + 128)
                    lhs[0, at, columns] = first[:, lanes]
                    lhs[1, at, columns] = second[:, lanes]

    def column_phase(part):
        columns = slice(part * 256, part * 256 + 256)
        above = slice(HALF + part * 256, HALF + part * 256 + 256)
        for second in range(2):
            table = txb if second else txa
            rc[...] = jnp.dot(lhs[second], table[:, columns], preferred_element_type=F32)
            rs[...] = jnp.dot(lhs[second], table[:, above], preferred_element_type=F32)

            @pl.loop(0, TM)
            def _(block):
                at = pl.ds(pl.multiple_of(block * 32, 32), 32)
                cosine = rc[at].reshape(4, 8, 256)
                sine = rs[at].reshape(4, 8, 256)
                top = lax.broadcasted_iota(jnp.int32, (4, 8, 256), 1) < 4
                swapped = pltpu.roll(sine, 4, 1)
                swapped = jnp.where(top, swapped, -swapped)
                plus, minus = cosine + swapped, cosine - swapped
                if part == 0:
                    edge = lax.broadcasted_iota(jnp.int32, (4, 8, 256), 2) == 0
                    plus = jnp.where(edge, cosine, plus)
                    minus = jnp.where(edge, sine, minus)
                modes[block, second, :, columns] = plus.reshape(32, 256).astype(BF16)
                modes[block, second, :, above] = minus.reshape(32, 256).astype(BF16)

    def window_at(window, columns):
        return modes[pl.ds(window, 2), :, :, columns].reshape(128, 256)

    def time_phase(slot, part):
        for half in range(2):
            columns = slice(half * HALF + part * 256, half * HALF + part * 256 + 256)
            total = None
            for window in range(TM - 1):
                u = jnp.dot(
                    time_ref[:128], window_at(window, columns), preferred_element_type=F32
                )
                u = u * u
                power = u[:64] + u[64:]
                total = power if total is None else total + power
            own_ref[slot, :, columns] = total
            msg[slot, part, :, half * 256 : half * 256 + 256] = total.astype(BF16)

        @pl.when((me == 0) & (slot == 0))
        def _():
            columns = slice(part * 256, part * 256 + 256)
            above = slice(HALF + part * 256, HALF + part * 256 + 256)
            lane = lax.broadcasted_iota(jnp.int32, (128, 256), 1) + part * 256
            sums = [None] * 4
            for window in range(TM - 1):
                a, b = (
                    jnp.dot(time_ref[...], window_at(window, at), preferred_element_type=F32)
                    for at in (columns, above)
                )
                back_a = jnp.where(lane == 0, a[128:], b[128:])
                back_b = jnp.where(lane == 0, b[128:], a[128:])
                terms = []
                for here, back in ((a[:128], back_a), (b[:128], back_b)):
                    r, i, rb, ib = here[:64], here[64:], back[:64], back[64:]
                    terms.append((r + rb) * (r + rb) + (i - ib) * (i - ib))
                    terms.append((r - rb) * (r - rb) + (i + ib) * (i + ib))
                sums = [t if s is None else s + t for s, t in zip(sums, terms)]
            own_ref[0, :, columns] = sums[0] * 0.25
            own_ref[0, :, above] = sums[2] * 0.25
            msg[0, part, :, :256] = (sums[1] * 0.25).astype(BF16)
            msg[0, part, :, 256:] = (sums[3] * 0.25).astype(BF16)

    def own_phase(slot):
        swap = (lax.broadcasted_iota(jnp.int32, (WIN, HALF), 1) >= 1) & (me >= 64)
        a, b = own_ref[slot, :, :HALF], own_ref[slot, :, HALF:]
        a, b = jnp.where(swap, b, a), jnp.where(swap, a, b)
        falling = jnp.dot(b.astype(BF16), flip[...], preferred_element_type=F32)
        stack[slot, :, :HALF] = a.astype(BF16)
        stack[slot, :, HALF:] = falling.astype(BF16)

    def own_copy(slot):
        return pltpu.make_async_copy(stack.at[slot], own_hbm.at[slot], own_sem.at[slot])

    mirror = DEVICES - 1 - me
    first_to = jnp.where(me == 0, 64, jnp.where(me < 64, DEVICES - me, mirror))

    def message(slot, part):
        target = jnp.where(slot == 0, first_to, mirror)
        return pltpu.make_async_remote_copy(
            src_ref=msg.at[slot, part],
            dst_ref=got_hbm.at[slot, part],
            send_sem=msg_send_sem.at[slot, part],
            recv_sem=msg_recv_sem.at[slot, part],
            device_id={"tm": target // ROWS, "rows": target % ROWS},
            device_id_type=MESH,
        )

    loads[0].wait()
    row_tables(0)
    row_phase(0)
    pl.semaphore_wait(barrier, DEVICES - 1)

    @pl.loop(0, SLOTS)
    def _(slot):
        start_sends(slot)

        @pl.when(slot == 0)
        def _():
            loads[1].wait()
            for other in range(1, SLOTS):
                row_tables(other)

        @pl.when(slot < SLOTS - 1)
        def _():
            row_phase(slot + 1)

    loads[2].wait()
    column_tables()
    make_flip(flip)

    @pl.loop(0, SLOTS)
    def _(slot):
        local_copy(slot).wait()
        wait_all(slot, recv_sem)
        gather_phase(slot)
        for part in range(2):
            column_phase(part)
            time_phase(slot, part)
            message(slot, part).start()
        own_phase(slot)
        own_copy(slot).start()

    @pl.loop(0, SLOTS)
    def _(slot):
        wait_all(slot, send_sem)
        own_copy(slot).wait()
        for part in range(2):
            message(slot, part).wait()


def final_kernel(
    scale, own_hbm, got_hbm, out_hbm, stack, got_ref, left, flip, result, in_sem, out_sem
):
    loads = [pltpu.make_async_copy(got_hbm, got_ref, in_sem.at[0])]
    for half in range(2):
        columns = pl.ds(half * HALF, HALF)
        loads.append(
            pltpu.make_async_copy(
                own_hbm.at[:, columns], stack.at[pl.ds(0, 256), columns], in_sem.at[1 + half]
            )
        )
    for load in loads:
        load.start()
    me = lax.axis_index("tm") * ROWS + lax.axis_index("rows")
    upper = me >= 64
    make_flip(flip)
    to = lax.broadcasted_iota(jnp.int32, (HALF, HALF), 0)
    come = lax.broadcasted_iota(jnp.int32, (HALF, HALF), 1)
    w, row = to // 8, to % 8
    mirrored = jnp.where(row == 0, 4, jnp.where(row <= 4, 4 - row, 12 - row))
    source = jnp.where(upper, mirrored * WIN + (WIN - w) % WIN, row * WIN + w)
    left[...] = jnp.where(come == source, 1.0, 0.0).astype(BF16)
    swap = (lax.broadcasted_iota(jnp.int32, (256, HALF), 1) >= 1) & upper

    stores = []

    def place(part):
        columns = slice(part * 256, part * 256 + 256)
        product = jnp.dot(left[...], stack[:, columns], preferred_element_type=F32) * scale
        result[part] = product.reshape(WIN, 8, 256)
        store = pltpu.make_async_copy(
            result.at[part], out_hbm.at[:, :, pl.ds(part * 256, 256)], out_sem.at[part]
        )
        store.start()
        stores.append(store)

    loads[0].wait()
    a, b = (
        jnp.concatenate(
            [got_ref[:, part, :, at].reshape(256, 256).astype(F32) for part in range(2)], 1
        )
        for at in (slice(0, 256), slice(256, 512))
    )
    stack[256:, :HALF] = jnp.where(swap, b, a).astype(BF16)
    loads[1].wait()
    place(0)
    place(1)
    falling = jnp.where(swap, a, b).astype(BF16)
    falling = jnp.dot(falling, flip[...], preferred_element_type=F32)
    stack[256:, HALF:] = falling.astype(BF16)
    loads[2].wait()
    place(2)
    place(3)
    for store in stores:
        store.wait()


def body(heights):
    vmem = pl.BlockSpec(memory_space=pltpu.VMEM)
    hbm = pl.BlockSpec(memory_space=pl.ANY)
    energy = tapers()[2]
    dma = pltpu.SemaphoreType.DMA
    own, got = pl.pallas_call(
        spectrum_kernel,
        out_shape=(
            jax.ShapeDtypeStruct((SLOTS, WIN, GRID), BF16),
            jax.ShapeDtypeStruct((SLOTS, 2, WIN, HALF), BF16),
        ),
        in_specs=[hbm] * 3 + [vmem],
        out_specs=(hbm, hbm),
        scratch_shapes=[
            pltpu.VMEM((FRAMES_DEV, X_DEV, GRID), BF16),
            pltpu.VMEM((SLOTS, QUARTER, HALF), BF16),
            pltpu.VMEM((HALF, GRID), BF16),
            pltpu.VMEM((SLOTS, WIN, GRID), F32),
            pltpu.VMEM((SLOTS, QUARTER, GRID), BF16),
            pltpu.VMEM((GRID, GRID), BF16),
            pltpu.VMEM((GRID, GRID), BF16),
            pltpu.VMEM((8, QUARTER, 256), F32),
            pltpu.VMEM((SLOTS, DEVICES // 4, 4, 16, 256), BF16),
            pltpu.VMEM((SLOTS, DEVICES, 16, 256), BF16),
            pltpu.VMEM((2, QUARTER, GRID), BF16),
            pltpu.VMEM((QUARTER, 256), F32),
            pltpu.VMEM((QUARTER, 256), F32),
            pltpu.VMEM((TM, 2, 32, GRID), BF16),
            pltpu.VMEM((SLOTS, 2, WIN, HALF), BF16),
            pltpu.VMEM((SLOTS, WIN, GRID), BF16),
            pltpu.VMEM((HALF, HALF), BF16),
            dma((SLOTS,)),
            dma((SLOTS,)),
            dma((SLOTS,)),
            dma((SLOTS, 2)),
            dma((SLOTS, 2)),
            dma((3,)),
            dma((8,)),
            dma((SLOTS,)),
        ],
        compiler_params=pltpu.CompilerParams(
            collective_id=0, has_side_effects=True, vmem_limit_bytes=VMEM_ALL
        ),
    )(
        heights,
        jnp.asarray(row_table()),
        jnp.asarray(column_table()),
        jnp.asarray(time_matrices()),
    )
    return pl.pallas_call(
        functools.partial(final_kernel, 1.0 / ((TM - 1) * energy)),
        out_shape=jax.ShapeDtypeStruct((WIN, 8, GRID), F32),
        in_specs=[hbm, hbm],
        out_specs=hbm,
        scratch_shapes=[
            pltpu.VMEM((HALF, GRID), BF16),
            pltpu.VMEM((SLOTS, 2, WIN, HALF), BF16),
            pltpu.VMEM((HALF, HALF), BF16),
            pltpu.VMEM((HALF, HALF), BF16),
            pltpu.VMEM((4, WIN, 8, 256), F32),
            dma((3,)),
            dma((4,)),
        ],
        compiler_params=pltpu.CompilerParams(vmem_limit_bytes=VMEM_ALL),
    )(own.reshape(256, GRID), got)


def solution(mesh):
    return jax.shard_map(
        body,
        mesh=mesh,
        in_specs=(P("tm", "rows", None),),
        out_specs=P(None, ("tm", "rows"), None),
        check_vma=False,
    )
```

```python
import functools
import math

import jax
import jax.numpy as jnp
import ml_dtypes
import numpy as np
from jax import lax
from jax.experimental import pallas as pl
from jax.experimental.pallas import tpu as pltpu
from jax.sharding import PartitionSpec as P

MESH = pl.DeviceIdType.MESH
GRID = 1024
HALF = 512
WIN = 64
TM = 8
ROWS = 16
DEVICES = TM * ROWS
FRAMES_DEV = 32
X_DEV = 64
SLOTS = 4
QUARTER = 256
VMEM_ALL = 67_000_000
BF16 = jnp.bfloat16
F32 = jnp.float32


def trig(index):
    angles = (index % GRID).astype(np.float32) * np.float32(2.0 * math.pi / GRID)
    scale = np.float32(math.sqrt(GRID))
    return np.cos(angles) / scale, np.sin(angles) / scale


def row_table():
    row = np.arange(QUARTER)
    quad, part, low = row // 8, row // 4 % 2, row % 4
    device = 4 * quad + low
    y = np.arange(HALF)
    tables = []
    for slot in range(SLOTS):
        q = np.where(device < 64, 8 * device + slot, 8 * (127 - device) + 4 + slot)
        cosine, sine = trig(q[:, None] * y[None, :])
        values = np.where(part[:, None] == 0, cosine, -sine)
        shared = (device == 0) & (slot == 0) & (part == 1)
        nyquist, _ = trig(HALF * y)
        tables.append(np.where(shared[:, None], nyquist[None, :], values))
    return np.stack(tables).astype(ml_dtypes.bfloat16)


def column_table():
    x = np.arange(HALF)
    cosine, sine = trig(x[:, None] * x[None, :])
    sine[:, 0] = trig(x * HALF)[0]
    return np.concatenate([cosine, sine], 1).astype(ml_dtypes.bfloat16)


def tapers():
    t = np.arange(WIN)
    hann = np.float32(0.5) - np.float32(0.5) * np.cos(
        t.astype(np.float32) * np.float32(2.0 * math.pi / WIN)
    )
    angles = (t[:, None] * t[None, :] % WIN).astype(np.float32) * np.float32(2.0 * math.pi / WIN)
    energy = float(np.sum(hann * hann, dtype=np.float32))

    def rounded(values):
        return (values * hann[None, :]).astype(ml_dtypes.bfloat16).astype(np.float32)

    return rounded(np.cos(angles)), rounded(np.sin(angles)), energy


def time_matrices():
    cosine, sine, _ = tapers()
    k = np.arange(128)
    block, second, inner = k // 64, k // 32 % 2, k // 16 % 2
    high, part, low = k // 8 % 2, k // 4 % 2, k % 4
    t = 32 * block + 16 * high + 4 * low + 2 * inner + second
    real = np.where(part == 0, cosine[:, t], sine[:, t])
    imag = np.where(part == 0, -sine[:, t], cosine[:, t])
    back = (-np.arange(WIN)) % WIN
    return np.concatenate([real, imag, real[back], imag[back]]).astype(ml_dtypes.bfloat16)


def far(step):
    a, b = step // ROWS, step % ROWS
    return min(a // 2, 4 - a // 2) + a % 2 * 2 + b // 8 + min(b // 2 % 4, 4 - b // 2 % 4)


def make_flip(flip):
    i = lax.broadcasted_iota(jnp.int32, (HALF, HALF), 0)
    j = lax.broadcasted_iota(jnp.int32, (HALF, HALF), 1)
    flip[...] = jnp.where(i == (HALF - j) % HALF, 1.0, 0.0).astype(BF16)


def spectrum_kernel(
    h_hbm, ty_hbm, tx_hbm, time_ref, own_hbm, got_hbm,
    h_ref, ty_ref, tx_ref, own_ref, tab, txa, txb, rowsum, send, recv, lhs, rc, rs, modes, msg, stack, flip,
    send_sem, recv_sem, local_sem, msg_send_sem, msg_recv_sem, load_sem, height_sem, own_sem,
):
    tm, rows = lax.axis_index("tm"), lax.axis_index("rows")
    me = tm * ROWS + rows
    x, y, z, core = tm // 2, rows // 2 % 4, tm % 2 * 2 + rows // 8, rows % 2

    def height_load(eighth):
        frames = pl.ds(eighth * 4, 4)
        return pltpu.make_async_copy(h_hbm.at[frames], h_ref.at[frames], height_sem.at[eighth])

    later = pl.ds(1, SLOTS - 1)
    loads = [
        pltpu.make_async_copy(ty_hbm.at[0], ty_ref.at[0], load_sem.at[0]),
        pltpu.make_async_copy(ty_hbm.at[later], ty_ref.at[later], load_sem.at[1]),
        pltpu.make_async_copy(tx_hbm, tx_ref, load_sem.at[2]),
    ]
    loads[0].start()
    for eighth in range(8):
        height_load(eighth).start()
    loads[1].start()
    loads[2].start()

    barrier = pltpu.get_barrier_semaphore()
    tm_of = [(tm + a) % TM for a in range(TM)]
    rows_of = [(rows + b) % ROWS for b in range(ROWS)]
    for step in sorted(range(1, DEVICES), key=far, reverse=True):
        pl.semaphore_signal(
            barrier,
            inc=1,
            device_id={"tm": tm_of[step // ROWS], "rows": rows_of[step % ROWS]},
            device_id_type=MESH,
        )

    def row_tables(slot):
        tab[slot, :, :HALF] = ty_ref[slot]
        tab[slot, :, HALF:] = -ty_ref[slot] if slot % 2 else ty_ref[slot]

    def column_tables():
        lane_sign = jnp.where(lax.broadcasted_iota(jnp.int32, (1, GRID), 1) % 2 == 0, 1.0, -1.0)
        txa[:HALF] = tx_ref[...]
        txa[HALF:] = (tx_ref[...].astype(F32) * lane_sign).astype(BF16)

        @pl.loop(0, 8)
        def _(block):
            base = pl.multiple_of(block * 128, 128)
            txb[pl.ds(base, 64)] = txa[pl.ds(base + 64, 64)]
            txb[pl.ds(base + 64, 64)] = txa[pl.ds(base, 64)]

    def row_phase(slot):
        first = isinstance(slot, int)

        @pl.loop(0, 8)
        def _(eighth):
            if first:
                height_load(eighth).wait()
            base = eighth * 4
            block = jnp.concatenate(
                [
                    h_ref[base + core],
                    h_ref[base + 1 - core],
                    h_ref[base + 2 + core],
                    h_ref[base + 3 - core],
                ],
                0,
            )
            rowsum[eighth] = lax.dot_general(
                tab[slot], block, (((1,), (1,)), ((), ())), preferred_element_type=F32
            )

        @pl.loop(0, 8)
        def _(part):
            at = pl.ds(pl.multiple_of(part * 32, 32), 32)
            row = lax.broadcasted_iota(jnp.int32, (4, 8, 256), 1)
            pair, single = row // 2 % 2 == 0, row % 2 == 0
            halves = []
            for high in range(2):
                r = [rowsum[4 * high + f, at].reshape(4, 8, 256) for f in range(4)]
                a = [None] * 4
                for f in range(2):
                    a[f] = jnp.where(pair, r[f], pltpu.roll(r[f + 2], 2, 1))
                    a[f + 2] = jnp.where(pair, pltpu.roll(r[f], 6, 1), r[f + 2])
                halves.append(
                    [
                        jnp.where(single, a[0], pltpu.roll(a[1], 1, 1)),
                        jnp.where(single, pltpu.roll(a[0], 7, 1), a[1]),
                        jnp.where(single, a[2], pltpu.roll(a[3], 1, 1)),
                        jnp.where(single, pltpu.roll(a[2], 7, 1), a[3]),
                    ]
                )
            for low in range(4):
                send[slot, pl.ds(part * 4, 4), low] = jnp.concatenate(
                    [halves[0][low], halves[1][low]], 1
                ).astype(BF16)

    def start_sends(slot):
        y_of = [(y + d) % 4 * 2 for d in range(4)]
        z_of = [(z + d) % 4 for d in range(4)]
        z_tm, z_rows = [v // 2 for v in z_of], [v % 2 * 8 for v in z_of]
        core_of = [core, 1 - core]

        @pl.loop(0, 4)
        def _(turn):
            x_of = [(x + 3 * turn + d) % 4 * 2 for d in range(4)]

            def start(step):
                shift = step * 107 % DEVICES
                to_tm = x_of[shift // 32] + z_tm[shift // 2 % 4]
                to_rows = z_rows[shift // 2 % 4] + y_of[shift // 8 % 4] + core_of[shift % 2]
                target = to_tm * ROWS + to_rows
                pltpu.make_async_remote_copy(
                    src_ref=send.at[slot, target // 4, target % 4],
                    dst_ref=recv.at[slot, me],
                    send_sem=send_sem.at[slot],
                    recv_sem=recv_sem.at[slot],
                    device_id={"tm": to_tm, "rows": to_rows},
                    device_id_type=MESH,
                ).start()

            @pl.when(turn > 0)
            def _():
                start(0)

            for step in range(1, 32):
                start(step)

        local_copy(slot).start()

    def local_copy(slot):
        return pltpu.make_async_copy(
            send.at[slot, me // 4, me % 4], recv.at[slot, me], local_sem.at[slot]
        )

    def wait_all(slot, sem):
        blocks = recv.at[slot, pl.ds(0, DEVICES - 1)]
        pltpu.make_async_copy(blocks, blocks, sem.at[slot]).wait()

    def gather_phase(slot):
        @pl.loop(0, TM)
        def _(block):
            low = lax.broadcasted_iota(jnp.int32, (16, 256), 1) % 128 < 64
            for pair in range(8):
                even = recv[slot, block * ROWS + 2 * pair]
                odd = recv[slot, block * ROWS + 2 * pair + 1]
                first = jnp.where(low, even, odd)
                second = jnp.where(low, odd, even)
                for inner in range(2):
                    at = pl.ds(pl.multiple_of(block * 32 + inner * 16, 16), 16)
                    lanes = slice(inner * 128, inner * 128 + 128)
                    columns = slice(pair * 128, pair * 128 + 128)
                    lhs[0, at, columns] = first[:, lanes]
                    lhs[1, at, columns] = second[:, lanes]

    def column_phase(part):
        columns = slice(part * 256, part * 256 + 256)
        above = slice(HALF + part * 256, HALF + part * 256 + 256)
        for second in range(2):
            table = txb if second else txa
            rc[...] = jnp.dot(lhs[second], table[:, columns], preferred_element_type=F32)
            rs[...] = jnp.dot(lhs[second], table[:, above], preferred_element_type=F32)

            @pl.loop(0, TM)
            def _(block):
                at = pl.ds(pl.multiple_of(block * 32, 32), 32)
                cosine = rc[at].reshape(4, 8, 256)
                sine = rs[at].reshape(4, 8, 256)
                top = lax.broadcasted_iota(jnp.int32, (4, 8, 256), 1) < 4
                swapped = pltpu.roll(sine, 4, 1)
                swapped = jnp.where(top, swapped, -swapped)
                plus, minus = cosine + swapped, cosine - swapped
                if part == 0:
                    edge = lax.broadcasted_iota(jnp.int32, (4, 8, 256), 2) == 0
                    plus = jnp.where(edge, cosine, plus)
                    minus = jnp.where(edge, sine, minus)
                modes[block, second, :, columns] = plus.reshape(32, 256).astype(BF16)
                modes[block, second, :, above] = minus.reshape(32, 256).astype(BF16)

    def window_at(window, columns):
        return modes[pl.ds(window, 2), :, :, columns].reshape(128, 256)

    def time_phase(slot, part):
        for half in range(2):
            columns = slice(half * HALF + part * 256, half * HALF + part * 256 + 256)
            total = None
            for window in range(TM - 1):
                u = jnp.dot(
                    time_ref[:128], window_at(window, columns), preferred_element_type=F32
                )
                u = u * u
                power = u[:64] + u[64:]
                total = power if total is None else total + power
            own_ref[slot, :, columns] = total
            msg[slot, part, :, half * 256 : half * 256 + 256] = total.astype(BF16)

        @pl.when((me == 0) & (slot == 0))
        def _():
            columns = slice(part * 256, part * 256 + 256)
            above = slice(HALF + part * 256, HALF + part * 256 + 256)
            lane = lax.broadcasted_iota(jnp.int32, (128, 256), 1) + part * 256
            sums = [None] * 4
            for window in range(TM - 1):
                a, b = (
                    jnp.dot(time_ref[...], window_at(window, at), preferred_element_type=F32)
                    for at in (columns, above)
                )
                back_a = jnp.where(lane == 0, a[128:], b[128:])
                back_b = jnp.where(lane == 0, b[128:], a[128:])
                terms = []
                for here, back in ((a[:128], back_a), (b[:128], back_b)):
                    r, i, rb, ib = here[:64], here[64:], back[:64], back[64:]
                    terms.append((r + rb) * (r + rb) + (i - ib) * (i - ib))
                    terms.append((r - rb) * (r - rb) + (i + ib) * (i + ib))
                sums = [t if s is None else s + t for s, t in zip(sums, terms)]
            own_ref[0, :, columns] = sums[0] * 0.25
            own_ref[0, :, above] = sums[2] * 0.25
            msg[0, part, :, :256] = (sums[1] * 0.25).astype(BF16)
            msg[0, part, :, 256:] = (sums[3] * 0.25).astype(BF16)

    def own_phase(slot):
        swap = (lax.broadcasted_iota(jnp.int32, (WIN, HALF), 1) >= 1) & (me >= 64)
        a, b = own_ref[slot, :, :HALF], own_ref[slot, :, HALF:]
        a, b = jnp.where(swap, b, a), jnp.where(swap, a, b)
        falling = jnp.dot(b.astype(BF16), flip[...], preferred_element_type=F32)
        stack[slot, :, :HALF] = a.astype(BF16)
        stack[slot, :, HALF:] = falling.astype(BF16)

    def own_copy(slot):
        return pltpu.make_async_copy(stack.at[slot], own_hbm.at[slot], own_sem.at[slot])

    mirror = DEVICES - 1 - me
    first_to = jnp.where(me == 0, 64, jnp.where(me < 64, DEVICES - me, mirror))

    def message(slot, part):
        target = jnp.where(slot == 0, first_to, mirror)
        return pltpu.make_async_remote_copy(
            src_ref=msg.at[slot, part],
            dst_ref=got_hbm.at[slot, part],
            send_sem=msg_send_sem.at[slot, part],
            recv_sem=msg_recv_sem.at[slot, part],
            device_id={"tm": target // ROWS, "rows": target % ROWS},
            device_id_type=MESH,
        )

    loads[0].wait()
    row_tables(0)
    row_phase(0)
    pl.semaphore_wait(barrier, DEVICES - 1)

    @pl.loop(0, SLOTS)
    def _(slot):
        start_sends(slot)

        @pl.when(slot == 0)
        def _():
            loads[1].wait()
            for other in range(1, SLOTS):
                row_tables(other)

        @pl.when(slot < SLOTS - 1)
        def _():
            row_phase(slot + 1)

    loads[2].wait()
    column_tables()
    make_flip(flip)

    @pl.loop(0, SLOTS)
    def _(slot):
        local_copy(slot).wait()
        wait_all(slot, recv_sem)
        gather_phase(slot)
        for part in range(2):
            column_phase(part)
            time_phase(slot, part)
            message(slot, part).start()
        own_phase(slot)
        own_copy(slot).start()

    @pl.loop(0, SLOTS)
    def _(slot):
        wait_all(slot, send_sem)
        own_copy(slot).wait()
        for part in range(2):
            message(slot, part).wait()


def final_kernel(
    scale, own_hbm, got_hbm, out_hbm, stack, got_ref, left, flip, result, in_sem, out_sem
):
    loads = [pltpu.make_async_copy(got_hbm, got_ref, in_sem.at[0])]
    for half in range(2):
        columns = pl.ds(half * HALF, HALF)
        loads.append(
            pltpu.make_async_copy(
                own_hbm.at[:, columns], stack.at[pl.ds(0, 256), columns], in_sem.at[1 + half]
            )
        )
    for load in loads:
        load.start()
    me = lax.axis_index("tm") * ROWS + lax.axis_index("rows")
    upper = me >= 64
    make_flip(flip)
    to = lax.broadcasted_iota(jnp.int32, (HALF, HALF), 0)
    come = lax.broadcasted_iota(jnp.int32, (HALF, HALF), 1)
    w, row = to // 8, to % 8
    mirrored = jnp.where(row == 0, 4, jnp.where(row <= 4, 4 - row, 12 - row))
    source = jnp.where(upper, mirrored * WIN + (WIN - w) % WIN, row * WIN + w)
    left[...] = jnp.where(come == source, 1.0, 0.0).astype(BF16)
    swap = (lax.broadcasted_iota(jnp.int32, (256, HALF), 1) >= 1) & upper

    stores = []

    def place(part):
        columns = slice(part * 256, part * 256 + 256)
        product = jnp.dot(left[...], stack[:, columns], preferred_element_type=F32) * scale
        result[part] = product.reshape(WIN, 8, 256)
        store = pltpu.make_async_copy(
            result.at[part], out_hbm.at[:, :, pl.ds(part * 256, 256)], out_sem.at[part]
        )
        store.start()
        stores.append(store)

    loads[0].wait()
    a, b = (
        jnp.concatenate(
            [got_ref[:, part, :, at].reshape(256, 256).astype(F32) for part in range(2)], 1
        )
        for at in (slice(0, 256), slice(256, 512))
    )
    stack[256:, :HALF] = jnp.where(swap, b, a).astype(BF16)
    loads[1].wait()
    place(0)
    place(1)
    falling = jnp.where(swap, a, b).astype(BF16)
    falling = jnp.dot(falling, flip[...], preferred_element_type=F32)
    stack[256:, HALF:] = falling.astype(BF16)
    loads[2].wait()
    place(2)
    place(3)
    for store in stores:
        store.wait()


def body(heights):
    vmem = pl.BlockSpec(memory_space=pltpu.VMEM)
    hbm = pl.BlockSpec(memory_space=pl.ANY)
    energy = tapers()[2]
    dma = pltpu.SemaphoreType.DMA
    own, got = pl.pallas_call(
        spectrum_kernel,
        out_shape=(
            jax.ShapeDtypeStruct((SLOTS, WIN, GRID), BF16),
            jax.ShapeDtypeStruct((SLOTS, 2, WIN, HALF), BF16),
        ),
        in_specs=[hbm] * 3 + [vmem],
        out_specs=(hbm, hbm),
        scratch_shapes=[
            pltpu.VMEM((FRAMES_DEV, X_DEV, GRID), BF16),
            pltpu.VMEM((SLOTS, QUARTER, HALF), BF16),
            pltpu.VMEM((HALF, GRID), BF16),
            pltpu.VMEM((SLOTS, WIN, GRID), F32),
            pltpu.VMEM((SLOTS, QUARTER, GRID), BF16),
            pltpu.VMEM((GRID, GRID), BF16),
            pltpu.VMEM((GRID, GRID), BF16),
            pltpu.VMEM((8, QUARTER, 256), F32),
            pltpu.VMEM((SLOTS, DEVICES // 4, 4, 16, 256), BF16),
            pltpu.VMEM((SLOTS, DEVICES, 16, 256), BF16),
            pltpu.VMEM((2, QUARTER, GRID), BF16),
            pltpu.VMEM((QUARTER, 256), F32),
            pltpu.VMEM((QUARTER, 256), F32),
            pltpu.VMEM((TM, 2, 32, GRID), BF16),
            pltpu.VMEM((SLOTS, 2, WIN, HALF), BF16),
            pltpu.VMEM((SLOTS, WIN, GRID), BF16),
            pltpu.VMEM((HALF, HALF), BF16),
            dma((SLOTS,)),
            dma((SLOTS,)),
            dma((SLOTS,)),
            dma((SLOTS, 2)),
            dma((SLOTS, 2)),
            dma((3,)),
            dma((8,)),
            dma((SLOTS,)),
        ],
        compiler_params=pltpu.CompilerParams(
            collective_id=0, has_side_effects=True, vmem_limit_bytes=VMEM_ALL
        ),
    )(
        heights,
        jnp.asarray(row_table()),
        jnp.asarray(column_table()),
        jnp.asarray(time_matrices()),
    )
    return pl.pallas_call(
        functools.partial(final_kernel, 1.0 / ((TM - 1) * energy)),
        out_shape=jax.ShapeDtypeStruct((WIN, 8, GRID), F32),
        in_specs=[hbm, hbm],
        out_specs=hbm,
        scratch_shapes=[
            pltpu.VMEM((HALF, GRID), BF16),
            pltpu.VMEM((SLOTS, 2, WIN, HALF), BF16),
            pltpu.VMEM((HALF, HALF), BF16),
            pltpu.VMEM((HALF, HALF), BF16),
            pltpu.VMEM((4, WIN, 8, 256), F32),
            dma((3,)),
            dma((4,)),
        ],
        compiler_params=pltpu.CompilerParams(vmem_limit_bytes=VMEM_ALL),
    )(own.reshape(256, GRID), got)


def solution(mesh):
    return jax.shard_map(
        body,
        mesh=mesh,
        in_specs=(P("tm", "rows", None),),
        out_specs=P(None, ("tm", "rows"), None),
        check_vma=False,
    )
```

```python
import functools
import math

import jax
import jax.numpy as jnp
import ml_dtypes
import numpy as np
from jax import lax
from jax.experimental import pallas as pl
from jax.experimental.pallas import tpu as pltpu
from jax.sharding import PartitionSpec as P

MESH = pl.DeviceIdType.MESH
GRID = 1024
HALF = 512
WIN = 64
TM = 8
ROWS = 16
DEVICES = TM * ROWS
FRAMES_DEV = 32
X_DEV = 64
SLOTS = 4
QUARTER = 256
VMEM_ALL = 67_000_000
BF16 = jnp.bfloat16
F32 = jnp.float32


def trig(index):
    angles = (index % GRID).astype(np.float32) * np.float32(2.0 * math.pi / GRID)
    scale = np.float32(math.sqrt(GRID))
    return np.cos(angles) / scale, np.sin(angles) / scale


def row_table():
    row = np.arange(QUARTER)
    quad, part, low = row // 8, row // 4 % 2, row % 4
    device = 4 * quad + low
    y = np.arange(HALF)
    tables = []
    for slot in range(SLOTS):
        q = np.where(device < 64, 8 * device + slot, 8 * (127 - device) + 4 + slot)
        cosine, sine = trig(q[:, None] * y[None, :])
        values = np.where(part[:, None] == 0, cosine, -sine)
        shared = (device == 0) & (slot == 0) & (part == 1)
        nyquist, _ = trig(HALF * y)
        tables.append(np.where(shared[:, None], nyquist[None, :], values))
    return np.stack(tables).astype(ml_dtypes.bfloat16)


def column_table():
    x = np.arange(HALF)
    cosine, sine = trig(x[:, None] * x[None, :])
    sine[:, 0] = trig(x * HALF)[0]
    return np.concatenate([cosine, sine], 1).astype(ml_dtypes.bfloat16)


def tapers():
    t = np.arange(WIN)
    hann = np.float32(0.5) - np.float32(0.5) * np.cos(
        t.astype(np.float32) * np.float32(2.0 * math.pi / WIN)
    )
    angles = (t[:, None] * t[None, :] % WIN).astype(np.float32) * np.float32(2.0 * math.pi / WIN)
    energy = float(np.sum(hann * hann, dtype=np.float32))

    def rounded(values):
        return (values * hann[None, :]).astype(ml_dtypes.bfloat16).astype(np.float32)

    return rounded(np.cos(angles)), rounded(np.sin(angles)), energy


def time_matrices():
    cosine, sine, _ = tapers()
    k = np.arange(128)
    block, second, inner = k // 64, k // 32 % 2, k // 16 % 2
    high, part, low = k // 8 % 2, k // 4 % 2, k % 4
    t = 32 * block + 16 * high + 4 * low + 2 * inner + second
    real = np.where(part == 0, cosine[:, t], sine[:, t])
    imag = np.where(part == 0, -sine[:, t], cosine[:, t])
    back = (-np.arange(WIN)) % WIN
    return np.concatenate([real, imag, real[back], imag[back]]).astype(ml_dtypes.bfloat16)


def far(step):
    a, b = step // ROWS, step % ROWS
    return min(a // 2, 4 - a // 2) + a % 2 * 2 + b // 8 + min(b // 2 % 4, 4 - b // 2 % 4)


def make_flip(flip):
    i = lax.broadcasted_iota(jnp.int32, (HALF, HALF), 0)
    j = lax.broadcasted_iota(jnp.int32, (HALF, HALF), 1)
    flip[...] = jnp.where(i == (HALF - j) % HALF, 1.0, 0.0).astype(BF16)


def spectrum_kernel(
    h_hbm, ty_hbm, tx_hbm, time_ref, own_hbm, got_hbm,
    h_ref, ty_ref, tx_ref, own_ref, tab, txa, txb, rowsum, send, recv, lhs, rc, rs, modes, msg, stack, flip,
    send_sem, recv_sem, local_sem, msg_send_sem, msg_recv_sem, load_sem, height_sem, own_sem,
):
    tm, rows = lax.axis_index("tm"), lax.axis_index("rows")
    me = tm * ROWS + rows
    x, y, z, core = tm // 2, rows // 2 % 4, tm % 2 * 2 + rows // 8, rows % 2

    def height_load(eighth):
        frames = pl.ds(eighth * 4, 4)
        return pltpu.make_async_copy(h_hbm.at[frames], h_ref.at[frames], height_sem.at[eighth])

    later = pl.ds(1, SLOTS - 1)
    loads = [
        pltpu.make_async_copy(ty_hbm.at[0], ty_ref.at[0], load_sem.at[0]),
        pltpu.make_async_copy(ty_hbm.at[later], ty_ref.at[later], load_sem.at[1]),
        pltpu.make_async_copy(tx_hbm, tx_ref, load_sem.at[2]),
    ]
    loads[0].start()
    for eighth in range(8):
        height_load(eighth).start()
    loads[1].start()
    loads[2].start()

    barrier = pltpu.get_barrier_semaphore()
    tm_of = [(tm + a) % TM for a in range(TM)]
    rows_of = [(rows + b) % ROWS for b in range(ROWS)]
    for step in sorted(range(1, DEVICES), key=far, reverse=True):
        pl.semaphore_signal(
            barrier,
            inc=1,
            device_id={"tm": tm_of[step // ROWS], "rows": rows_of[step % ROWS]},
            device_id_type=MESH,
        )

    def row_tables(slot):
        tab[slot, :, :HALF] = ty_ref[slot]
        tab[slot, :, HALF:] = -ty_ref[slot] if slot % 2 else ty_ref[slot]

    def column_tables():
        lane_sign = jnp.where(lax.broadcasted_iota(jnp.int32, (1, GRID), 1) % 2 == 0, 1.0, -1.0)
        txa[:HALF] = tx_ref[...]
        txa[HALF:] = (tx_ref[...].astype(F32) * lane_sign).astype(BF16)

        @pl.loop(0, 8)
        def _(block):
            base = pl.multiple_of(block * 128, 128)
            txb[pl.ds(base, 64)] = txa[pl.ds(base + 64, 64)]
            txb[pl.ds(base + 64, 64)] = txa[pl.ds(base, 64)]

    def row_phase(slot):
        first = isinstance(slot, int)

        @pl.loop(0, 8)
        def _(eighth):
            if first:
                height_load(eighth).wait()
            base = eighth * 4
            block = jnp.concatenate(
                [
                    h_ref[base + core],
                    h_ref[base + 1 - core],
                    h_ref[base + 2 + core],
                    h_ref[base + 3 - core],
                ],
                0,
            )
            rowsum[eighth] = lax.dot_general(
                tab[slot], block, (((1,), (1,)), ((), ())), preferred_element_type=F32
            )

        @pl.loop(0, 8)
        def _(part):
            at = pl.ds(pl.multiple_of(part * 32, 32), 32)
            row = lax.broadcasted_iota(jnp.int32, (4, 8, 256), 1)
            pair, single = row // 2 % 2 == 0, row % 2 == 0
            halves = []
            for high in range(2):
                r = [rowsum[4 * high + f, at].reshape(4, 8, 256) for f in range(4)]
                a = [None] * 4
                for f in range(2):
                    a[f] = jnp.where(pair, r[f], pltpu.roll(r[f + 2], 2, 1))
                    a[f + 2] = jnp.where(pair, pltpu.roll(r[f], 6, 1), r[f + 2])
                halves.append(
                    [
                        jnp.where(single, a[0], pltpu.roll(a[1], 1, 1)),
                        jnp.where(single, pltpu.roll(a[0], 7, 1), a[1]),
                        jnp.where(single, a[2], pltpu.roll(a[3], 1, 1)),
                        jnp.where(single, pltpu.roll(a[2], 7, 1), a[3]),
                    ]
                )
            for low in range(4):
                send[slot, pl.ds(part * 4, 4), low] = jnp.concatenate(
                    [halves[0][low], halves[1][low]], 1
                ).astype(BF16)

    def start_sends(slot):
        y_of = [(y + d) % 4 * 2 for d in range(4)]
        z_of = [(z + d) % 4 for d in range(4)]
        z_tm, z_rows = [v // 2 for v in z_of], [v % 2 * 8 for v in z_of]
        core_of = [core, 1 - core]

        @pl.loop(0, 4)
        def _(turn):
            x_of = [(x + 3 * turn + d) % 4 * 2 for d in range(4)]

            def start(step):
                shift = step * 11 % DEVICES
                to_tm = x_of[shift // 32] + z_tm[shift // 2 % 4]
                to_rows = z_rows[shift // 2 % 4] + y_of[shift // 8 % 4] + core_of[shift % 2]
                target = to_tm * ROWS + to_rows
                pltpu.make_async_remote_copy(
                    src_ref=send.at[slot, target // 4, target % 4],
                    dst_ref=recv.at[slot, me],
                    send_sem=send_sem.at[slot],
                    recv_sem=recv_sem.at[slot],
                    device_id={"tm": to_tm, "rows": to_rows},
                    device_id_type=MESH,
                ).start()

            @pl.when(turn > 0)
            def _():
                start(0)

            for step in range(1, 32):
                start(step)

        local_copy(slot).start()

    def local_copy(slot):
        return pltpu.make_async_copy(
            send.at[slot, me // 4, me % 4], recv.at[slot, me], local_sem.at[slot]
        )

    def wait_all(slot, sem):
        blocks = recv.at[slot, pl.ds(0, DEVICES - 1)]
        pltpu.make_async_copy(blocks, blocks, sem.at[slot]).wait()

    def gather_phase(slot):
        @pl.loop(0, TM)
        def _(block):
            low = lax.broadcasted_iota(jnp.int32, (16, 256), 1) % 128 < 64
            for pair in range(8):
                even = recv[slot, block * ROWS + 2 * pair]
                odd = recv[slot, block * ROWS + 2 * pair + 1]
                first = jnp.where(low, even, odd)
                second = jnp.where(low, odd, even)
                for inner in range(2):
                    at = pl.ds(pl.multiple_of(block * 32 + inner * 16, 16), 16)
                    lanes = slice(inner * 128, inner * 128 + 128)
                    columns = slice(pair * 128, pair * 128 + 128)
                    lhs[0, at, columns] = first[:, lanes]
                    lhs[1, at, columns] = second[:, lanes]

    def column_phase(part):
        columns = slice(part * 256, part * 256 + 256)
        above = slice(HALF + part * 256, HALF + part * 256 + 256)
        for second in range(2):
            table = txb if second else txa
            rc[...] = jnp.dot(lhs[second], table[:, columns], preferred_element_type=F32)
            rs[...] = jnp.dot(lhs[second], table[:, above], preferred_element_type=F32)

            @pl.loop(0, TM)
            def _(block):
                at = pl.ds(pl.multiple_of(block * 32, 32), 32)
                cosine = rc[at].reshape(4, 8, 256)
                sine = rs[at].reshape(4, 8, 256)
                top = lax.broadcasted_iota(jnp.int32, (4, 8, 256), 1) < 4
                swapped = pltpu.roll(sine, 4, 1)
                swapped = jnp.where(top, swapped, -swapped)
                plus, minus = cosine + swapped, cosine - swapped
                if part == 0:
                    edge = lax.broadcasted_iota(jnp.int32, (4, 8, 256), 2) == 0
                    plus = jnp.where(edge, cosine, plus)
                    minus = jnp.where(edge, sine, minus)
                modes[block, second, :, columns] = plus.reshape(32, 256).astype(BF16)
                modes[block, second, :, above] = minus.reshape(32, 256).astype(BF16)

    def window_at(window, columns):
        return modes[pl.ds(window, 2), :, :, columns].reshape(128, 256)

    def time_phase(slot, part):
        for half in range(2):
            columns = slice(half * HALF + part * 256, half * HALF + part * 256 + 256)
            total = None
            for window in range(TM - 1):
                u = jnp.dot(
                    time_ref[:128], window_at(window, columns), preferred_element_type=F32
                )
                u = u * u
                power = u[:64] + u[64:]
                total = power if total is None else total + power
            own_ref[slot, :, columns] = total
            msg[slot, part, :, half * 256 : half * 256 + 256] = total.astype(BF16)

        @pl.when((me == 0) & (slot == 0))
        def _():
            columns = slice(part * 256, part * 256 + 256)
            above = slice(HALF + part * 256, HALF + part * 256 + 256)
            lane = lax.broadcasted_iota(jnp.int32, (128, 256), 1) + part * 256
            sums = [None] * 4
            for window in range(TM - 1):
                a, b = (
                    jnp.dot(time_ref[...], window_at(window, at), preferred_element_type=F32)
                    for at in (columns, above)
                )
                back_a = jnp.where(lane == 0, a[128:], b[128:])
                back_b = jnp.where(lane == 0, b[128:], a[128:])
                terms = []
                for here, back in ((a[:128], back_a), (b[:128], back_b)):
                    r, i, rb, ib = here[:64], here[64:], back[:64], back[64:]
                    terms.append((r + rb) * (r + rb) + (i - ib) * (i - ib))
                    terms.append((r - rb) * (r - rb) + (i + ib) * (i + ib))
                sums = [t if s is None else s + t for s, t in zip(sums, terms)]
            own_ref[0, :, columns] = sums[0] * 0.25
            own_ref[0, :, above] = sums[2] * 0.25
            msg[0, part, :, :256] = (sums[1] * 0.25).astype(BF16)
            msg[0, part, :, 256:] = (sums[3] * 0.25).astype(BF16)

    def own_phase(slot):
        swap = (lax.broadcasted_iota(jnp.int32, (WIN, HALF), 1) >= 1) & (me >= 64)
        a, b = own_ref[slot, :, :HALF], own_ref[slot, :, HALF:]
        a, b = jnp.where(swap, b, a), jnp.where(swap, a, b)
        falling = jnp.dot(b.astype(BF16), flip[...], preferred_element_type=F32)
        stack[slot, :, :HALF] = a.astype(BF16)
        stack[slot, :, HALF:] = falling.astype(BF16)

    def own_copy(slot):
        return pltpu.make_async_copy(stack.at[slot], own_hbm.at[slot], own_sem.at[slot])

    mirror = DEVICES - 1 - me
    first_to = jnp.where(me == 0, 64, jnp.where(me < 64, DEVICES - me, mirror))

    def message(slot, part):
        target = jnp.where(slot == 0, first_to, mirror)
        return pltpu.make_async_remote_copy(
            src_ref=msg.at[slot, part],
            dst_ref=got_hbm.at[slot, part],
            send_sem=msg_send_sem.at[slot, part],
            recv_sem=msg_recv_sem.at[slot, part],
            device_id={"tm": target // ROWS, "rows": target % ROWS},
            device_id_type=MESH,
        )

    loads[0].wait()
    row_tables(0)
    row_phase(0)
    pl.semaphore_wait(barrier, DEVICES - 1)

    @pl.loop(0, SLOTS)
    def _(slot):
        start_sends(slot)

        @pl.when(slot == 0)
        def _():
            loads[1].wait()
            for other in range(1, SLOTS):
                row_tables(other)

        @pl.when(slot < SLOTS - 1)
        def _():
            row_phase(slot + 1)

    loads[2].wait()
    column_tables()
    make_flip(flip)

    @pl.loop(0, SLOTS)
    def _(slot):
        local_copy(slot).wait()
        wait_all(slot, recv_sem)
        gather_phase(slot)
        for part in range(2):
            column_phase(part)
            time_phase(slot, part)
            message(slot, part).start()
        own_phase(slot)
        own_copy(slot).start()

    @pl.loop(0, SLOTS)
    def _(slot):
        wait_all(slot, send_sem)
        own_copy(slot).wait()
        for part in range(2):
            message(slot, part).wait()


def final_kernel(
    scale, own_hbm, got_hbm, out_hbm, stack, got_ref, left, flip, result, in_sem, out_sem
):
    loads = [pltpu.make_async_copy(got_hbm, got_ref, in_sem.at[0])]
    for half in range(2):
        columns = pl.ds(half * HALF, HALF)
        loads.append(
            pltpu.make_async_copy(
                own_hbm.at[:, columns], stack.at[pl.ds(0, 256), columns], in_sem.at[1 + half]
            )
        )
    for load in loads:
        load.start()
    me = lax.axis_index("tm") * ROWS + lax.axis_index("rows")
    upper = me >= 64
    make_flip(flip)
    to = lax.broadcasted_iota(jnp.int32, (HALF, HALF), 0)
    come = lax.broadcasted_iota(jnp.int32, (HALF, HALF), 1)
    w, row = to // 8, to % 8
    mirrored = jnp.where(row == 0, 4, jnp.where(row <= 4, 4 - row, 12 - row))
    source = jnp.where(upper, mirrored * WIN + (WIN - w) % WIN, row * WIN + w)
    left[...] = jnp.where(come == source, 1.0, 0.0).astype(BF16)
    swap = (lax.broadcasted_iota(jnp.int32, (256, HALF), 1) >= 1) & upper

    stores = []

    def place(part):
        columns = slice(part * 256, part * 256 + 256)
        product = jnp.dot(left[...], stack[:, columns], preferred_element_type=F32) * scale
        result[part] = product.reshape(WIN, 8, 256)
        store = pltpu.make_async_copy(
            result.at[part], out_hbm.at[:, :, pl.ds(part * 256, 256)], out_sem.at[part]
        )
        store.start()
        stores.append(store)

    loads[0].wait()
    a, b = (
        jnp.concatenate(
            [got_ref[:, part, :, at].reshape(256, 256).astype(F32) for part in range(2)], 1
        )
        for at in (slice(0, 256), slice(256, 512))
    )
    stack[256:, :HALF] = jnp.where(swap, b, a).astype(BF16)
    loads[1].wait()
    place(0)
    place(1)
    falling = jnp.where(swap, a, b).astype(BF16)
    falling = jnp.dot(falling, flip[...], preferred_element_type=F32)
    stack[256:, HALF:] = falling.astype(BF16)
    loads[2].wait()
    place(2)
    place(3)
    for store in stores:
        store.wait()


def body(heights):
    vmem = pl.BlockSpec(memory_space=pltpu.VMEM)
    hbm = pl.BlockSpec(memory_space=pl.ANY)
    energy = tapers()[2]
    dma = pltpu.SemaphoreType.DMA
    own, got = pl.pallas_call(
        spectrum_kernel,
        out_shape=(
            jax.ShapeDtypeStruct((SLOTS, WIN, GRID), BF16),
            jax.ShapeDtypeStruct((SLOTS, 2, WIN, HALF), BF16),
        ),
        in_specs=[hbm] * 3 + [vmem],
        out_specs=(hbm, hbm),
        scratch_shapes=[
            pltpu.VMEM((FRAMES_DEV, X_DEV, GRID), BF16),
            pltpu.VMEM((SLOTS, QUARTER, HALF), BF16),
            pltpu.VMEM((HALF, GRID), BF16),
            pltpu.VMEM((SLOTS, WIN, GRID), F32),
            pltpu.VMEM((SLOTS, QUARTER, GRID), BF16),
            pltpu.VMEM((GRID, GRID), BF16),
            pltpu.VMEM((GRID, GRID), BF16),
            pltpu.VMEM((8, QUARTER, 256), F32),
            pltpu.VMEM((SLOTS, DEVICES // 4, 4, 16, 256), BF16),
            pltpu.VMEM((SLOTS, DEVICES, 16, 256), BF16),
            pltpu.VMEM((2, QUARTER, GRID), BF16),
            pltpu.VMEM((QUARTER, 256), F32),
            pltpu.VMEM((QUARTER, 256), F32),
            pltpu.VMEM((TM, 2, 32, GRID), BF16),
            pltpu.VMEM((SLOTS, 2, WIN, HALF), BF16),
            pltpu.VMEM((SLOTS, WIN, GRID), BF16),
            pltpu.VMEM((HALF, HALF), BF16),
            dma((SLOTS,)),
            dma((SLOTS,)),
            dma((SLOTS,)),
            dma((SLOTS, 2)),
            dma((SLOTS, 2)),
            dma((3,)),
            dma((8,)),
            dma((SLOTS,)),
        ],
        compiler_params=pltpu.CompilerParams(
            collective_id=0, has_side_effects=True, vmem_limit_bytes=VMEM_ALL
        ),
    )(
        heights,
        jnp.asarray(row_table()),
        jnp.asarray(column_table()),
        jnp.asarray(time_matrices()),
    )
    return pl.pallas_call(
        functools.partial(final_kernel, 1.0 / ((TM - 1) * energy)),
        out_shape=jax.ShapeDtypeStruct((WIN, 8, GRID), F32),
        in_specs=[hbm, hbm],
        out_specs=hbm,
        scratch_shapes=[
            pltpu.VMEM((HALF, GRID), BF16),
            pltpu.VMEM((SLOTS, 2, WIN, HALF), BF16),
            pltpu.VMEM((HALF, HALF), BF16),
            pltpu.VMEM((HALF, HALF), BF16),
            pltpu.VMEM((4, WIN, 8, 256), F32),
            dma((3,)),
            dma((4,)),
        ],
        compiler_params=pltpu.CompilerParams(vmem_limit_bytes=VMEM_ALL),
    )(own.reshape(256, GRID), got)


def solution(mesh):
    return jax.shard_map(
        body,
        mesh=mesh,
        in_specs=(P("tm", "rows", None),),
        out_specs=P(None, ("tm", "rows"), None),
        check_vma=False,
    )
```
